32 devices in a mesh: field: 2 (over x), focus: 2 (over core), strip: 8 (over z, y).
Axes of the slice: x: 2, y: 2, z: 4, core: 2. Of those that a mesh axis runs over, the one named last changes fastest.
Arguments:
- slices: bfloat16 [32, 4096, 4096], P(('field', 'focus'), 'strip'), parts along dimension 0, may hold values from 0 to 1
- otf_rows: float32 [4096], replicated, may hold values from 0.1 to 1
- otf_cols: float32 [4096], replicated, may hold values from 0.1 to 1
Outputs:
- restored: float32 [8192, 4096], P(('field', 'focus', 'strip')), parts along dimension 0
The draws below stay inside these ranges and needn't reach their ends.
There are 2 independent parts, one for each index of `field`. The reference program is written for one: setup_inputs(seed, part) draws one part's arguments, and reference() takes and returns one part's arrays. A program takes and returns all parts, laid end to end along the dimension named above; an argument that names none is the same for every part. Nothing has to cross between parts.
All inputs are finite; a program needn't handle non-finite values.
Results may differ from the reference program's by a relative error of at most 0.011.
Values may be sent and summed in bfloat16 or wider, within the bound.
No kernel may reach another device: no remote copies, remote signals or barrier semaphores. Data moves between devices by JAX's collectives and lax.ppermute only.
A program may use at most 256 MiB of HBM per device.

```python
import math
import jax
import jax.numpy as jnp
from jax import lax

N = 4096
SLICES = 16


def steps_of(key, extent, pieces, least, largest):
    level, own = 1.0, jax.random.fold_in(key, 6)
    for axis_at, blocks in pieces:
        draws = jnp.exp(jax.random.uniform(jax.random.fold_in(own, axis_at), (blocks,), jnp.float32, least / len(pieces), largest / len(pieces)))
        level = level * jnp.repeat(draws, extent[axis_at] // blocks).reshape([-1 if axis == axis_at else 1 for axis in range(len(extent))])
    return level


def setup_inputs(seed: int = 0, part: int = 0) -> dict:
    key_list = jax.random.split(jax.random.key(seed), 4)
    part_keys = jax.random.split(jax.random.fold_in(key_list[3], part), 4)
    return {
        "slices": jnp.clip(1.0 * jax.random.uniform(part_keys[0], (SLICES, N, N), jnp.float32) ** steps_of(part_keys[0], (SLICES, N, N), ((0, 2), (1, 8)), -0.2, 0.2), 0.0, 1.0).astype(jnp.bfloat16),
        "otf_rows": jnp.clip(jnp.exp(jax.random.uniform(key_list[1], (N,), jnp.float32, math.log(0.1), math.log(1.0))), 0.1, 1.0),
        "otf_cols": jnp.clip(jnp.exp(jax.random.uniform(key_list[2], (N,), jnp.float32, math.log(0.1), math.log(1.0))), 0.1, 1.0),
    }


floor_weight = 0.01
noise_ratio = 0.01

def cosine_block(first_row, height, length):
    low_count = min(64, length)
    high_count = length // low_count
    frequency = first_row + lax.broadcasted_iota(jnp.int32, (height, 1), 0)
    high_sample = lax.broadcasted_iota(jnp.int32, (1, high_count), 1)
    low_sample = lax.broadcasted_iota(jnp.int32, (1, low_count), 1)
    high_phase = 2 * low_count * high_sample * frequency % (4 * length)
    low_phase = (2 * low_sample + 1) * frequency % (4 * length)
    unit = jnp.float32(math.pi / (2 * length))
    high_angle = high_phase.astype(jnp.float32) * unit
    low_angle = low_phase.astype(jnp.float32) * unit
    norming = jnp.where(frequency == 0, jnp.float32(math.sqrt(1.0 / length)), jnp.float32(math.sqrt(2.0 / length)))
    high_cos = (norming * jnp.cos(high_angle))[:, :, None]
    high_sin = (norming * jnp.sin(high_angle))[:, :, None]
    low_cos = jnp.cos(low_angle)[:, None, :]
    low_sin = jnp.sin(low_angle)[:, None, :]
    table = high_cos * low_cos - high_sin * low_sin
    return table.reshape(height, length).astype(jnp.bfloat16)

def cosine_table(length):
    height = min(512, length)
    starts = jnp.arange(length // height, dtype=jnp.int32) * height
    return lax.map(lambda first_row: cosine_block(first_row, height, length), starts).reshape(length, length)

def laplace(picture, spacing):
    padded = jnp.pad(picture, spacing)
    total = padded[2 * spacing:, spacing:-spacing] + padded[:-2 * spacing, spacing:-spacing]
    total = total + padded[spacing:-spacing, 2 * spacing:] + padded[spacing:-spacing, :-2 * spacing]
    return total - 4.0 * picture

def matmul(left, right):
    return jnp.dot(left.astype(jnp.float32), right.astype(jnp.float32), precision=lax.Precision.HIGHEST)

def reference(slices, otf_rows, otf_cols):

    def add_slice(totals, slice_plane):
        numerator, denominator = totals
        picture = slice_plane.astype(jnp.float32)
        fine_term = laplace(picture, 1)
        middle_term = laplace(picture, 2)
        coarse_term = laplace(picture, 4)
        weight = floor_weight + fine_term * fine_term + 0.5 * middle_term * middle_term + 0.25 * coarse_term * coarse_term
        return ((numerator + weight * picture, denominator + weight), None)
    blank_field = jnp.zeros((N, N), jnp.float32)
    (numerator, denominator), _ = lax.scan(add_slice, (blank_field, blank_field), slices)
    merged_field = (numerator / denominator).astype(jnp.bfloat16)
    cosines = cosine_table(N)
    along_cols = matmul(merged_field, cosines.T).astype(jnp.bfloat16)
    spectrum = matmul(cosines, along_cols)
    response = otf_rows[:, None] * otf_cols[None, :]
    filtered = (spectrum * (response / (response * response + noise_ratio))).astype(jnp.bfloat16)
    back_cols = matmul(cosines.T, filtered).astype(jnp.bfloat16)
    return matmul(back_cols, cosines)
```

```python
import functools
import math

import jax
import jax.numpy as jnp
from jax import lax
from jax.experimental import pallas as pl
from jax.experimental.pallas import tpu as pltpu
from jax.sharding import PartitionSpec as P

floor_weight = 0.01
noise_ratio = 0.01
lane_block = 256
row_chunks = 2


def dot(left, right):
    return jnp.dot(left, right, preferred_element_type=jnp.float32)


def dot_last(left, right):
    return lax.dot_general(left, right, (((1,), (1,)), ((), ())), preferred_element_type=jnp.float32)


def edge_rows(slices, width):
    count = lax.axis_size("strip")
    ends = count - 1
    head = slices[:, :width, :]
    tail = slices[:, slices.shape[1] - width :, :]
    above = lax.ppermute(tail, "strip", [(i, i + 1) for i in range(ends)])
    below = lax.ppermute(head, "strip", [(i + 1, i) for i in range(ends)])
    return above, below


def band():
    source = lax.broadcasted_iota(jnp.int32, (256, 512), 0)
    column = lax.broadcasted_iota(jnp.int32, (256, 512), 1)
    which = column // 128
    offset = source - column % 128 - 64
    spacing = jnp.where(which == 0, 1, jnp.where(which == 1, 2, 4))
    lap = jnp.where(offset == 0, -4.0, jnp.where(jnp.abs(offset) == spacing, 1.0, 0.0))
    return jnp.where(which == 3, jnp.where(offset == 0, 1.0, 0.0), lap).astype(jnp.bfloat16)


def exchange_matrix():
    row = lax.broadcasted_iota(jnp.int32, (lane_block, lane_block), 0)
    column = lax.broadcasted_iota(jnp.int32, (lane_block, lane_block), 1)
    return (row + column == lane_block - 1).astype(jnp.bfloat16)


def stencil_kernel(
    place, main, above, below, head, tail, weights, out,
    edges, copies_a, copies_b, laps_a, laps_b, held,
    *, tile_rows, count, cols, tiles, step, parts,
):
    tile = place[0] + pl.program_id(0)
    first = tile == 0
    last = tile == tiles - 1
    edge_row = lax.broadcasted_iota(jnp.int32, (16, cols), 0)
    lane = lax.broadcasted_iota(jnp.int32, (step, 128), 1)
    for s in range(count):
        upper = jnp.where(first, head[s], above[s])
        lower = jnp.where(last, tail[s], below[s])
        edges[s] = jnp.where(edge_row < 8, lower, upper)
    frames = cols // 128 + 1
    copies = (copies_a, copies_b)
    laps = (laps_a, laps_b)

    def start_of(frame):
        return frame * 128 - 128 if isinstance(frame, int) else pl.multiple_of(frame * 128 - 128, 128)

    def window(source, frame, rows, low, high):
        size = (high - low) * rows
        if isinstance(frame, int) and frame == 0:
            piece = source[low:high, :, pl.ds(0, 128)].reshape(size, 128)
            return jnp.concatenate([jnp.zeros_like(piece), piece], axis=1)
        if isinstance(frame, int) and frame == frames - 1:
            piece = source[low:high, :, pl.ds(cols - 128, 128)].reshape(size, 128)
            return jnp.concatenate([piece, jnp.zeros_like(piece)], axis=1)
        return source[low:high, :, pl.ds(start_of(frame), 256)].reshape(size, 256)

    def spread_edges(slot, frame):
        rows = dot(window(edges, frame, 16, 0, count), weights[:, pl.ds(384, 128)])
        for s in range(count):
            copies[slot][s, pl.ds(0, 8), :] = rows[16 * s + 8 : 16 * s + 16]
            copies[slot][s, pl.ds(8 + tile_rows, 8), :] = rows[16 * s : 16 * s + 8]

    def spread(slot, frame, low, high):
        rows = dot(window(main, frame, tile_rows, low, high), weights[...])
        for s in range(low, high):
            at = (s - low) * tile_rows
            copies[slot][s, pl.ds(8, tile_rows), :] = rows[at : at + tile_rows, 384:]
            for k in range(3):
                laps[slot][s, k] = rows[at : at + tile_rows, 128 * k : 128 * k + 128]

    def gather(slot, frame, low, high):
        for r in range(low, high, step):
            numerator = jnp.zeros((step, 128), jnp.float32)
            denominator = numerator
            for s in range(count):
                centers = copies[slot]

                def lap(k, d):
                    pair = centers[s, pl.ds(8 + r + d, step), :] + centers[s, pl.ds(8 + r - d, step), :]
                    return laps[slot][s, k, pl.ds(r, step), :] + pair

                fine, middle, coarse = lap(0, 1), lap(1, 2), lap(2, 4)
                weight = floor_weight + (
                    fine * fine + 0.5 * (middle * middle + 0.5 * (coarse * coarse))
                )
                numerator += weight * centers[s, pl.ds(8 + r, step), :]
                denominator += weight
            for k, value in enumerate((numerator, denominator)):
                turned = pltpu.roll(value, 64, 1)
                if not (isinstance(frame, int) and frame == 0):
                    joined = jnp.where(lane < 64, held[k, pl.ds(r, step), :], turned)
                    out[k, pl.ds(r, step), pl.ds(start_of(frame), 128)] = joined
                held[k, pl.ds(r, step), :] = turned

    def both(slot, frame):
        spread_edges(slot, frame)
        for q in range(parts):
            spread(slot, frame, q * count // parts, (q + 1) * count // parts)
            gather(1 - slot, frame - 1, q * tile_rows // parts, (q + 1) * tile_rows // parts)

    spread_edges(0, 0)
    spread(0, 0, 0, count)
    both(1, 1)
    both(0, 2)

    def two(i, carry):
        both(1, 2 * i + 1)
        both(0, 2 * i + 2)
        return carry

    lax.fori_loop(1, frames // 2 - 1, two, 0)
    both(1, frames - 2)
    both(0, frames - 1)
    gather(0, frames - 1, 0, tile_rows)


def stencil(place, slices, head, tail, weights, out_rows):
    count, rows, cols = slices.shape
    tile_rows = math.gcd(128, out_rows)
    per = tile_rows // 16
    blocks = rows // 16
    step = min(16, tile_rows)
    parts = math.gcd(math.gcd(4, count), tile_rows // step)
    kernel = functools.partial(
        stencil_kernel, tile_rows=tile_rows, count=count, cols=cols, tiles=rows // tile_rows, step=step, parts=parts
    )
    edge = (count, 16, cols)
    grid_spec = pltpu.PrefetchScalarGridSpec(
        num_scalar_prefetch=1,
        grid=(out_rows // tile_rows,),
        in_specs=[
            pl.BlockSpec((count, tile_rows, cols), lambda t, at: (0, at[0] + t, 0)),
            pl.BlockSpec(edge, lambda t, at: (0, jnp.maximum((at[0] + t) * per - 1, 0), 0)),
            pl.BlockSpec(edge, lambda t, at: (0, jnp.minimum((at[0] + t) * per + per, blocks - 1), 0)),
            pl.BlockSpec(edge, lambda t, at: (0, 0, 0)),
            pl.BlockSpec(edge, lambda t, at: (0, 0, 0)),
            pl.BlockSpec((256, 512), lambda t, at: (0, 0)),
        ],
        out_specs=pl.BlockSpec((2, tile_rows, cols), lambda t, at: (0, t, 0)),
        scratch_shapes=[
            pltpu.VMEM(edge, jnp.bfloat16),
            pltpu.VMEM((count, tile_rows + 16, 128), jnp.float32),
            pltpu.VMEM((count, tile_rows + 16, 128), jnp.float32),
            pltpu.VMEM((count, 3, tile_rows, 128), jnp.float32),
            pltpu.VMEM((count, 3, tile_rows, 128), jnp.float32),
            pltpu.VMEM((2, tile_rows, 128), jnp.float32),
        ],
    )
    pixels = count * out_rows * cols
    return pl.pallas_call(
        kernel,
        grid_spec=grid_spec,
        out_shape=jax.ShapeDtypeStruct((2, out_rows, cols), jnp.float32),
        cost_estimate=pl.CostEstimate(flops=pixels * 2048, bytes_accessed=pixels * 3, transcendentals=0),
        compiler_params=pltpu.CompilerParams(vmem_limit_bytes=60 << 20),
        name="stencil",
    )(place, slices, slices, slices, head, tail, weights)


def table_kernel(near, turn, far, out, *, half):
    near_cos, near_sin = near[0, 0], near[0, 1]
    turn_cos, turn_sin = turn[0, 0], turn[0, 1]
    low_cos = near_cos * turn_cos - near_sin * turn_sin
    low_sin = near_sin * turn_cos + near_cos * turn_sin
    shape = low_cos.shape
    for j in range(half // 128):
        high_cos = jnp.broadcast_to(far[0, 0, :, j : j + 1], shape)
        high_sin = jnp.broadcast_to(far[0, 1, :, j : j + 1], shape)
        out[0, :, pl.ds(j * 128, 128)] = (high_cos * low_cos - high_sin * low_sin).astype(jnp.bfloat16)


def cosine_halves(length):
    half = length // 2
    rows = min(256, half)
    unit = jnp.float32(math.pi / (2 * length))

    def pair(phase, scale):
        angle = (phase % (4 * length)).astype(jnp.float32) * unit
        return jnp.stack([jnp.cos(angle) * scale, jnp.sin(angle) * scale], axis=1)

    def iota(shape, dim):
        return lax.broadcasted_iota(jnp.int32, shape, dim)

    odd = (2, rows, 128)
    near = pair((2 * iota(odd, 2) + 1) * (2 * iota(odd, 1) + iota(odd, 0)), 1.0)
    blocks = (half // rows, 1, 128)
    turn = pair((2 * iota(blocks, 2) + 1) * (2 * rows * iota(blocks, 0)), 1.0)
    steps = (2, half, half // 128)
    frequency = 2 * iota(steps, 1) + iota(steps, 0)
    norming = jnp.where(
        frequency == 0, jnp.float32(math.sqrt(1.0 / length)), jnp.float32(math.sqrt(2.0 / length))
    )
    far = pair(256 * iota(steps, 2) * frequency, norming)
    return pl.pallas_call(
        functools.partial(table_kernel, half=half),
        grid=(2, half // rows),
        in_specs=[
            pl.BlockSpec((1, 2, rows, 128), lambda p, b: (p, 0, 0, 0)),
            pl.BlockSpec((1, 2, 1, 128), lambda p, b: (b, 0, 0, 0)),
            pl.BlockSpec((1, 2, rows, half // 128), lambda p, b: (p, 0, b, 0)),
        ],
        out_specs=pl.BlockSpec((1, rows, half), lambda p, b: (p, b, 0)),
        out_shape=jax.ShapeDtypeStruct((2, half, half), jnp.bfloat16),
        name="cosines",
    )(near, turn, far)


def merge_kernel(own, other, mirror, out, *, cols):
    def merged(at):
        numerator = own[0, :, pl.ds(at, lane_block)] + other[0, :, pl.ds(at, lane_block)]
        denominator = own[1, :, pl.ds(at, lane_block)] + other[1, :, pl.ds(at, lane_block)]
        return (numerator / denominator).astype(jnp.bfloat16)

    for at in range(0, cols // 2, lane_block):
        near = merged(at).astype(jnp.float32)
        far = dot(merged(cols - lane_block - at), mirror[...])
        out[0, :, pl.ds(at, lane_block)] = (near + far).astype(jnp.bfloat16)
        out[1, :, pl.ds(at, lane_block)] = (near - far).astype(jnp.bfloat16)


def merge(own, other, mirror):
    _, rows, cols = own.shape
    tile = min(64, rows)
    return pl.pallas_call(
        functools.partial(merge_kernel, cols=cols),
        grid=(rows // tile,),
        in_specs=[
            pl.BlockSpec((2, tile, cols), lambda t: (0, t, 0)),
            pl.BlockSpec((2, tile, cols), lambda t: (0, t, 0)),
            pl.BlockSpec((lane_block, lane_block), lambda t: (0, 0)),
        ],
        out_specs=pl.BlockSpec((2, tile, cols // 2), lambda t: (0, t, 0)),
        out_shape=jax.ShapeDtypeStruct((2, rows, cols // 2), jnp.bfloat16),
        name="merge",
    )(own, other, mirror)


def rows_kernel(table, folded, out):
    values = dot_last(table[0], folded[0]).astype(jnp.bfloat16)
    out[...] = values.reshape(out.shape)


def transform_rows(table, folded, parity, devices):
    _, rows, half = folded.shape
    own = half // devices
    tile = max(256, own)
    return pl.pallas_call(
        rows_kernel,
        grid=(half // tile,),
        in_specs=[
            pl.BlockSpec((1, tile, half), lambda t: (parity, t, 0)),
            pl.BlockSpec((1, rows, half), lambda t: (parity, 0, 0)),
        ],
        out_specs=pl.BlockSpec((tile // own, own, rows), lambda t: (t, 0, 0)),
        out_shape=jax.ShapeDtypeStruct((devices, own, rows), jnp.bfloat16),
        name="transform_rows",
    )(table, folded)


def columns_kernel(*refs, chunks, half, order):
    table, rows_response, cols_response, mirror = refs[:4]
    arrived = refs[4 : 4 + chunks]
    out, folded, total = refs[4 + chunks :]
    parity = pl.program_id(0)
    step = pl.program_id(1)
    blocks = half // lane_block

    @pl.when((parity == 0) & (step == 0))
    def _():
        for j in range(blocks):
            near = jnp.concatenate([part[order[j]] for part in arrived], axis=1).astype(jnp.float32)
            far = dot(
                jnp.concatenate([part[order[2 * blocks - 1 - j]] for part in arrived], axis=1), mirror[...]
            )
            folded[0, :, pl.ds(j * lane_block, lane_block)] = (near + far).astype(jnp.bfloat16)
            folded[1, :, pl.ds(j * lane_block, lane_block)] = (near - far).astype(jnp.bfloat16)

    spectrum = dot_last(folded[parity], table[0])
    response = cols_response[...] * rows_response[0]
    filtered = (spectrum * (response / (response * response + noise_ratio))).astype(jnp.bfloat16)
    part = dot(filtered, table[0])

    @pl.when(step == 0)
    def _():
        total[parity] = part

    @pl.when(step > 0)
    def _():
        total[parity] += part

    @pl.when((parity == 1) & (step == pl.num_programs(1) - 1))
    def _():
        for j in range(blocks):
            even = total[0, :, pl.ds(j * lane_block, lane_block)]
            odd = total[1, :, pl.ds(j * lane_block, lane_block)]
            out[j] = (even + odd).astype(jnp.bfloat16)
            out[2 * blocks - 1 - j] = dot((even - odd).astype(jnp.bfloat16), mirror[...]).astype(jnp.bfloat16)


def filter_columns(table, rows_response, cols_response, mirror, arrived, order):
    half = table.shape[1]
    blocks, own, _ = arrived[0].shape
    tile = min(256, half)
    chunks = len(arrived)
    whole = pl.BlockSpec((blocks, own, lane_block // chunks), lambda p, t: (0, 0, 0))
    return pl.pallas_call(
        functools.partial(columns_kernel, chunks=chunks, half=half, order=order),
        grid=(2, half // tile),
        in_specs=[
            pl.BlockSpec((1, tile, half), lambda p, t: (p, t, 0)),
            pl.BlockSpec((1, 1, tile), lambda p, t: (p, 0, t)),
            pl.BlockSpec((own, 1), lambda p, t: (0, 0)),
            pl.BlockSpec((lane_block, lane_block), lambda p, t: (0, 0)),
        ]
        + [whole] * chunks,
        out_specs=pl.BlockSpec((blocks, own, lane_block), lambda p, t: (0, 0, 0)),
        out_shape=jax.ShapeDtypeStruct((blocks, own, lane_block), jnp.bfloat16),
        scratch_shapes=[
            pltpu.VMEM((2, own, half), jnp.bfloat16),
            pltpu.VMEM((2, own, half), jnp.float32),
        ],
        compiler_params=pltpu.CompilerParams(vmem_limit_bytes=60 << 20),
        name="filter_columns",
    )(table, rows_response, cols_response, mirror, *arrived)


def turn(values):
    return jnp.transpose(values.astype(jnp.float32)).astype(jnp.bfloat16)


def even_kernel(table, arrived, out, turned, *, half):
    @pl.when(pl.program_id(0) == 0)
    def _():
        rows = arrived.shape[2]
        turned[...] = turn(arrived[...].reshape(half, rows))

    out[...] = dot(turned[...], table[0])


def restore_even(table, arrived):
    half = table.shape[1]
    devices, own, rows = arrived.shape
    tile = min(256, half)
    return pl.pallas_call(
        functools.partial(even_kernel, half=half),
        grid=(half // tile,),
        in_specs=[
            pl.BlockSpec((1, half, tile), lambda t: (0, 0, t)),
            pl.BlockSpec((devices, own, rows), lambda t: (0, 0, 0)),
        ],
        out_specs=pl.BlockSpec((rows, tile), lambda t: (0, t)),
        out_shape=jax.ShapeDtypeStruct((rows, half), jnp.float32),
        scratch_shapes=[pltpu.VMEM((rows, half), jnp.bfloat16)],
        compiler_params=pltpu.CompilerParams(vmem_limit_bytes=60 << 20),
        name="restore_even",
    )(table, arrived)


def odd_kernel(table, arrived, even, mirror, out, turned, *, half, tile):
    step = pl.program_id(0)

    @pl.when(step == 0)
    def _():
        rows = arrived.shape[2]
        turned[...] = turn(arrived[...].reshape(half, rows))

    odd = dot(turned[...], table[0])
    out[:, pl.ds(pl.multiple_of(step * tile, tile), tile)] = even[...] + odd
    left = even[...] - odd
    back = jnp.zeros_like(left)
    for _ in range(3):
        piece = left.astype(jnp.bfloat16)
        back += dot(piece, mirror[...])
        left = left - piece.astype(jnp.float32)
    out[:, pl.ds(pl.multiple_of(2 * half - tile - step * tile, tile), tile)] = back


def restore(table, arrived, even, mirror):
    half = table.shape[1]
    devices, own, rows = arrived.shape
    tile = lane_block
    return pl.pallas_call(
        functools.partial(odd_kernel, half=half, tile=tile),
        grid=(half // tile,),
        in_specs=[
            pl.BlockSpec((1, half, tile), lambda t: (1, 0, t)),
            pl.BlockSpec((devices, own, rows), lambda t: (0, 0, 0)),
            pl.BlockSpec((rows, tile), lambda t: (0, t)),
            pl.BlockSpec((lane_block, lane_block), lambda t: (0, 0)),
        ],
        out_specs=pl.BlockSpec((rows, 2 * half), lambda t: (0, 0)),
        out_shape=jax.ShapeDtypeStruct((rows, 2 * half), jnp.float32),
        scratch_shapes=[pltpu.VMEM((rows, half), jnp.bfloat16)],
        compiler_params=pltpu.CompilerParams(vmem_limit_bytes=60 << 20),
        name="restore",
    )(table, arrived, even, mirror)


def body(slices, otf_rows, otf_cols):
    axes = ("focus", "strip")
    focus_count = lax.axis_size("focus")
    devices = focus_count * lax.axis_size("strip")
    rows, length = slices.shape[1:]
    half = length // 2
    piece = length // devices
    above, below = edge_rows(slices, 4)
    table = cosine_halves(length)
    head = jnp.pad(above, ((0, 0), (12, 0), (0, 0)))
    tail = jnp.pad(below, ((0, 0), (0, 12), (0, 0)))
    weights = band()
    mirror = exchange_matrix()
    focus = lax.axis_index("focus")
    chunks = row_chunks if piece % (16 * row_chunks) == 0 else 1
    if piece // chunks * chunks != piece or piece < lane_block:
        chunks = 1
    chunk_rows = piece // chunks
    tile_rows = math.gcd(128, chunk_rows)
    swap = [(i, focus_count - 1 - i) for i in range(focus_count)]
    arrived = ([], [])
    for chunk in range(chunks):
        def sums(half_index):
            place = (half_index * piece + chunk * chunk_rows) // tile_rows
            return stencil(place.astype(jnp.int32).reshape(1), slices, head, tail, weights, chunk_rows)

        sent = sums(focus_count - 1 - focus)
        received = lax.ppermute(sent, "focus", swap)
        own = sums(focus)
        folded = merge(own, received, mirror)
        for parity in range(2):
            along = transform_rows(table, folded, parity, devices)
            moved = lax.all_to_all(along, axes, split_axis=0, concat_axis=0, tiled=True)
            arrived[parity].append(moved)
    blocks = length // lane_block
    per = lane_block // piece
    owner = focus * lax.axis_size("strip") + lax.axis_index("strip")
    own = half // devices
    rows_response = otf_rows.reshape(half, 2).T.reshape(2, 1, half)
    local_cols = lax.dynamic_slice_in_dim(otf_cols.reshape(half, 2), owner * own, own, 0)
    strips = devices // focus_count
    order = [b % focus_count * strips + b // focus_count if per == 1 else b for b in range(blocks)]
    restored = []
    for parity in range(2):
        parts = arrived[parity]
        if per > 1:
            parts = [
                part.reshape(focus_count, devices // focus_count, own, piece)
                .transpose(1, 0, 2, 3)
                .reshape(blocks, per, own, piece)
                .transpose(0, 2, 1, 3)
                .reshape(blocks, own, lane_block)
                for part in parts
            ]
        back = filter_columns(table, rows_response, local_cols[:, parity : parity + 1], mirror, parts, order)
        if per > 1:
            back = back.reshape(blocks, own, per, piece).transpose(0, 2, 1, 3).reshape(devices, own, piece)
        restored.append(lax.all_to_all(back, axes, split_axis=0, concat_axis=0, tiled=True))
    even = restore_even(table, restored[0])
    return restore(table, restored[1], even, mirror)


def solution(mesh):
    in_specs = (P(("field", "focus"), "strip", None), P(), P())
    out_specs = P(("field", "focus", "strip"), None)
    return jax.shard_map(body, mesh=mesh, in_specs=in_specs, out_specs=out_specs, check_vma=False)
```

```python
import functools
import math

import jax
import jax.numpy as jnp
from jax import lax
from jax.experimental import pallas as pl
from jax.experimental.pallas import tpu as pltpu
from jax.sharding import PartitionSpec as P

floor_weight = 0.01
noise_ratio = 0.01
lane_block = 256
row_chunks = 2


def dot(left, right):
    return jnp.dot(left, right, preferred_element_type=jnp.float32)


def dot_last(left, right):
    return lax.dot_general(left, right, (((1,), (1,)), ((), ())), preferred_element_type=jnp.float32)


def edge_rows(slices, width):
    count = lax.axis_size("strip")
    ends = count - 1
    head = slices[:, :width, :]
    tail = slices[:, slices.shape[1] - width :, :]
    above = lax.ppermute(tail, "strip", [(i, i + 1) for i in range(ends)])
    below = lax.ppermute(head, "strip", [(i + 1, i) for i in range(ends)])
    return above, below


def band():
    source = lax.broadcasted_iota(jnp.int32, (256, 512), 0)
    column = lax.broadcasted_iota(jnp.int32, (256, 512), 1)
    which = column // 128
    offset = source - column % 128 - 64
    spacing = jnp.where(which == 0, 1, jnp.where(which == 1, 2, 4))
    lap = jnp.where(offset == 0, -4.0, jnp.where(jnp.abs(offset) == spacing, 1.0, 0.0))
    return jnp.where(which == 3, jnp.where(offset == 0, 1.0, 0.0), lap).astype(jnp.bfloat16)


def exchange_matrix():
    row = lax.broadcasted_iota(jnp.int32, (lane_block, lane_block), 0)
    column = lax.broadcasted_iota(jnp.int32, (lane_block, lane_block), 1)
    return (row + column == lane_block - 1).astype(jnp.bfloat16)


def stencil_kernel(
    place, main, above, below, head, tail, weights, out,
    edges, copies_a, copies_b, laps_a, laps_b, held,
    *, tile_rows, count, cols, tiles, step, parts,
):
    tile = place[0] + pl.program_id(0)
    first = tile == 0
    last = tile == tiles - 1
    edge_row = lax.broadcasted_iota(jnp.int32, (16, cols), 0)
    lane = lax.broadcasted_iota(jnp.int32, (step, 128), 1)
    for s in range(count):
        upper = jnp.where(first, head[s], above[s])
        lower = jnp.where(last, tail[s], below[s])
        edges[s] = jnp.where(edge_row < 8, lower, upper)
    frames = cols // 128 + 1
    copies = (copies_a, copies_b)
    laps = (laps_a, laps_b)

    def start_of(frame):
        return frame * 128 - 128 if isinstance(frame, int) else pl.multiple_of(frame * 128 - 128, 128)

    def window(source, frame, rows, low, high):
        size = (high - low) * rows
        if isinstance(frame, int) and frame == 0:
            piece = source[low:high, :, pl.ds(0, 128)].reshape(size, 128)
            return jnp.concatenate([jnp.zeros_like(piece), piece], axis=1)
        if isinstance(frame, int) and frame == frames - 1:
            piece = source[low:high, :, pl.ds(cols - 128, 128)].reshape(size, 128)
            return jnp.concatenate([piece, jnp.zeros_like(piece)], axis=1)
        return source[low:high, :, pl.ds(start_of(frame), 256)].reshape(size, 256)

    def spread_edges(slot, frame):
        rows = dot(window(edges, frame, 16, 0, count), weights[:, pl.ds(384, 128)])
        for s in range(count):
            copies[slot][s, pl.ds(0, 8), :] = rows[16 * s + 8 : 16 * s + 16]
            copies[slot][s, pl.ds(8 + tile_rows, 8), :] = rows[16 * s : 16 * s + 8]

    def spread(slot, frame, low, high):
        rows = dot(window(main, frame, tile_rows, low, high), weights[...])
        for s in range(low, high):
            at = (s - low) * tile_rows
            copies[slot][s, pl.ds(8, tile_rows), :] = rows[at : at + tile_rows, 384:]
            for k in range(3):
                laps[slot][s, k] = rows[at : at + tile_rows, 128 * k : 128 * k + 128]

    def gather(slot, frame, low, high):
        for r in range(low, high, step):
            numerator = jnp.zeros((step, 128), jnp.float32)
            denominator = numerator
            for s in range(count):
                centers = copies[slot]

                def lap(k, d):
                    pair = centers[s, pl.ds(8 + r + d, step), :] + centers[s, pl.ds(8 + r - d, step), :]
                    return laps[slot][s, k, pl.ds(r, step), :] + pair

                fine, middle, coarse = lap(0, 1), lap(1, 2), lap(2, 4)
                weight = floor_weight + (
                    fine * fine + 0.5 * (middle * middle + 0.5 * (coarse * coarse))
                )
                numerator += weight * centers[s, pl.ds(8 + r, step), :]
                denominator += weight
            for k, value in enumerate((numerator, denominator)):
                turned = pltpu.roll(value, 64, 1)
                if not (isinstance(frame, int) and frame == 0):
                    joined = jnp.where(lane < 64, held[k, pl.ds(r, step), :], turned)
                    out[k, pl.ds(r, step), pl.ds(start_of(frame), 128)] = joined
                held[k, pl.ds(r, step), :] = turned

    def both(slot, frame):
        spread_edges(slot, frame)
        for q in range(parts):
            spread(slot, frame, q * count // parts, (q + 1) * count // parts)
            gather(1 - slot, frame - 1, q * tile_rows // parts, (q + 1) * tile_rows // parts)

    spread_edges(0, 0)
    spread(0, 0, 0, count)
    both(1, 1)
    both(0, 2)

    def two(i, carry):
        both(1, 2 * i + 1)
        both(0, 2 * i + 2)
        return carry

    lax.fori_loop(1, frames // 2 - 1, two, 0)
    both(1, frames - 2)
    both(0, frames - 1)
    gather(0, frames - 1, 0, tile_rows)


def stencil(place, slices, head, tail, weights, out_rows):
    count, rows, cols = slices.shape
    tile_rows = math.gcd(128, out_rows)
    per = tile_rows // 16
    blocks = rows // 16
    step = min(16, tile_rows)
    parts = math.gcd(math.gcd(4, count), tile_rows // step)
    kernel = functools.partial(
        stencil_kernel, tile_rows=tile_rows, count=count, cols=cols, tiles=rows // tile_rows, step=step, parts=parts
    )
    edge = (count, 16, cols)
    grid_spec = pltpu.PrefetchScalarGridSpec(
        num_scalar_prefetch=1,
        grid=(out_rows // tile_rows,),
        in_specs=[
            pl.BlockSpec((count, tile_rows, cols), lambda t, at: (0, at[0] + t, 0)),
            pl.BlockSpec(edge, lambda t, at: (0, jnp.maximum((at[0] + t) * per - 1, 0), 0)),
            pl.BlockSpec(edge, lambda t, at: (0, jnp.minimum((at[0] + t) * per + per, blocks - 1), 0)),
            pl.BlockSpec(edge, lambda t, at: (0, 0, 0)),
            pl.BlockSpec(edge, lambda t, at: (0, 0, 0)),
            pl.BlockSpec((256, 512), lambda t, at: (0, 0)),
        ],
        out_specs=pl.BlockSpec((2, tile_rows, cols), lambda t, at: (0, t, 0)),
        scratch_shapes=[
            pltpu.VMEM(edge, jnp.bfloat16),
            pltpu.VMEM((count, tile_rows + 16, 128), jnp.float32),
            pltpu.VMEM((count, tile_rows + 16, 128), jnp.float32),
            pltpu.VMEM((count, 3, tile_rows, 128), jnp.float32),
            pltpu.VMEM((count, 3, tile_rows, 128), jnp.float32),
            pltpu.VMEM((2, tile_rows, 128), jnp.float32),
        ],
    )
    pixels = count * out_rows * cols
    return pl.pallas_call(
        kernel,
        grid_spec=grid_spec,
        out_shape=jax.ShapeDtypeStruct((2, out_rows, cols), jnp.float32),
        cost_estimate=pl.CostEstimate(flops=pixels * 2048, bytes_accessed=pixels * 3, transcendentals=0),
        compiler_params=pltpu.CompilerParams(vmem_limit_bytes=60 << 20),
        name="stencil",
    )(place, slices, slices, slices, head, tail, weights)


def table_kernel(near, turn, step, out, *, half):
    parity, block = pl.program_id(0), pl.program_id(1)
    group = min(64, out.shape[1])
    norm = math.sqrt(1.0 / half)
    for at in range(0, out.shape[1], group):
        rows = pl.ds(at, group)
        near_cos, near_sin = near[0, 0, rows, :], near[0, 1, rows, :]
        low_cos = near_cos * turn[0, 0] - near_sin * turn[0, 1]
        low_sin = near_sin * turn[0, 0] + near_cos * turn[0, 1]
        step_cos = jnp.broadcast_to(step[0, rows, 0:1], low_cos.shape)
        step_sin = jnp.broadcast_to(step[0, rows, 1:2], low_cos.shape)
        row = at + lax.broadcasted_iota(jnp.int32, low_cos.shape, 0)
        first = (row == 0) & (parity == 0) & (block == 0)
        scale = jnp.where(first, norm * math.sqrt(0.5), norm)
        before = scale * low_cos
        here = scale * (step_cos * low_cos - step_sin * low_sin)
        twice = step_cos + step_cos
        out[0, rows, pl.ds(0, 128)] = before.astype(jnp.bfloat16)
        for j in range(1, half // 128):
            out[0, rows, pl.ds(j * 128, 128)] = here.astype(jnp.bfloat16)
            before, here = here, twice * here - before


def cosine_halves(length):
    half = length // 2
    rows = min(256, half)
    unit = jnp.float32(math.pi / (2 * length))

    def pair(phase, axis):
        angle = (phase % (4 * length)).astype(jnp.float32) * unit
        return jnp.stack([jnp.cos(angle), jnp.sin(angle)], axis=axis)

    def iota(shape, dim):
        return lax.broadcasted_iota(jnp.int32, shape, dim)

    odd = (2, rows, 128)
    near = pair((2 * iota(odd, 2) + 1) * (2 * iota(odd, 1) + iota(odd, 0)), 1)
    blocks = (half // rows, 1, 128)
    turn = pair((2 * iota(blocks, 2) + 1) * (2 * rows * iota(blocks, 0)), 1)
    steps = (2, half)
    step = pair(256 * (2 * iota(steps, 1) + iota(steps, 0)), 2)
    return pl.pallas_call(
        functools.partial(table_kernel, half=half),
        grid=(2, half // rows),
        in_specs=[
            pl.BlockSpec((1, 2, rows, 128), lambda p, b: (p, 0, 0, 0)),
            pl.BlockSpec((1, 2, 1, 128), lambda p, b: (b, 0, 0, 0)),
            pl.BlockSpec((1, rows, 2), lambda p, b: (p, b, 0)),
        ],
        out_specs=pl.BlockSpec((1, rows, half), lambda p, b: (p, b, 0)),
        out_shape=jax.ShapeDtypeStruct((2, half, half), jnp.bfloat16),
        name="cosines",
    )(near, turn, step)


def merge_kernel(own, other, mirror, out, *, cols):
    def merged(at):
        numerator = own[0, :, pl.ds(at, lane_block)] + other[0, :, pl.ds(at, lane_block)]
        denominator = own[1, :, pl.ds(at, lane_block)] + other[1, :, pl.ds(at, lane_block)]
        return (numerator / denominator).astype(jnp.bfloat16)

    for at in range(0, cols // 2, lane_block):
        near = merged(at).astype(jnp.float32)
        far = dot(merged(cols - lane_block - at), mirror[...])
        out[0, :, pl.ds(at, lane_block)] = (near + far).astype(jnp.bfloat16)
        out[1, :, pl.ds(at, lane_block)] = (near - far).astype(jnp.bfloat16)


def merge(own, other, mirror):
    _, rows, cols = own.shape
    tile = min(64, rows)
    return pl.pallas_call(
        functools.partial(merge_kernel, cols=cols),
        grid=(rows // tile,),
        in_specs=[
            pl.BlockSpec((2, tile, cols), lambda t: (0, t, 0)),
            pl.BlockSpec((2, tile, cols), lambda t: (0, t, 0)),
            pl.BlockSpec((lane_block, lane_block), lambda t: (0, 0)),
        ],
        out_specs=pl.BlockSpec((2, tile, cols // 2), lambda t: (0, t, 0)),
        out_shape=jax.ShapeDtypeStruct((2, rows, cols // 2), jnp.bfloat16),
        name="merge",
    )(own, other, mirror)


def rows_kernel(table, folded, out):
    values = dot_last(table[0], folded[0]).astype(jnp.bfloat16)
    out[...] = values.reshape(out.shape)


def transform_rows(table, folded, parity, devices):
    _, rows, half = folded.shape
    own = half // devices
    tile = max(512, own)
    return pl.pallas_call(
        rows_kernel,
        grid=(half // tile,),
        in_specs=[
            pl.BlockSpec((1, tile, half), lambda t: (parity, t, 0)),
            pl.BlockSpec((1, rows, half), lambda t: (parity, 0, 0)),
        ],
        out_specs=pl.BlockSpec((tile // own, own, rows), lambda t: (t, 0, 0)),
        out_shape=jax.ShapeDtypeStruct((devices, own, rows), jnp.bfloat16),
        name="transform_rows",
    )(table, folded)


def columns_kernel(*refs, chunks, half, order):
    table, rows_response, cols_response, mirror = refs[:4]
    arrived = refs[4 : 4 + chunks]
    out, folded, total = refs[4 + chunks :]
    parity = pl.program_id(0)
    step = pl.program_id(1)
    blocks = half // lane_block

    @pl.when((parity == 0) & (step == 0))
    def _():
        for j in range(blocks):
            near = jnp.concatenate([part[order[j]] for part in arrived], axis=1).astype(jnp.float32)
            far = dot(
                jnp.concatenate([part[order[2 * blocks - 1 - j]] for part in arrived], axis=1), mirror[...]
            )
            folded[0, :, pl.ds(j * lane_block, lane_block)] = (near + far).astype(jnp.bfloat16)
            folded[1, :, pl.ds(j * lane_block, lane_block)] = (near - far).astype(jnp.bfloat16)

    spectrum = dot_last(folded[parity], table[0])
    response = cols_response[...] * rows_response[0]
    filtered = (spectrum * (response / (response * response + noise_ratio))).astype(jnp.bfloat16)
    part = dot(filtered, table[0])

    @pl.when(step == 0)
    def _():
        total[parity] = part

    @pl.when(step > 0)
    def _():
        total[parity] += part

    @pl.when((parity == 1) & (step == pl.num_programs(1) - 1))
    def _():
        for j in range(blocks):
            even = total[0, :, pl.ds(j * lane_block, lane_block)]
            odd = total[1, :, pl.ds(j * lane_block, lane_block)]
            out[j] = (even + odd).astype(jnp.bfloat16)
            out[2 * blocks - 1 - j] = dot((even - odd).astype(jnp.bfloat16), mirror[...]).astype(jnp.bfloat16)


def filter_columns(table, rows_response, cols_response, mirror, arrived, order):
    half = table.shape[1]
    blocks, own, _ = arrived[0].shape
    tile = min(512, half)
    chunks = len(arrived)
    whole = pl.BlockSpec((blocks, own, lane_block // chunks), lambda p, t: (0, 0, 0))
    return pl.pallas_call(
        functools.partial(columns_kernel, chunks=chunks, half=half, order=order),
        grid=(2, half // tile),
        in_specs=[
            pl.BlockSpec((1, tile, half), lambda p, t: (p, t, 0)),
            pl.BlockSpec((1, 1, tile), lambda p, t: (p, 0, t)),
            pl.BlockSpec((own, 1), lambda p, t: (0, 0)),
            pl.BlockSpec((lane_block, lane_block), lambda p, t: (0, 0)),
        ]
        + [whole] * chunks,
        out_specs=pl.BlockSpec((blocks, own, lane_block), lambda p, t: (0, 0, 0)),
        out_shape=jax.ShapeDtypeStruct((blocks, own, lane_block), jnp.bfloat16),
        scratch_shapes=[
            pltpu.VMEM((2, own, half), jnp.bfloat16),
            pltpu.VMEM((2, own, half), jnp.float32),
        ],
        compiler_params=pltpu.CompilerParams(vmem_limit_bytes=60 << 20),
        name="filter_columns",
    )(table, rows_response, cols_response, mirror, *arrived)


def turn(values):
    return jnp.transpose(values.astype(jnp.float32)).astype(jnp.bfloat16)


def even_kernel(table, arrived, out, turned, *, half):
    @pl.when(pl.program_id(0) == 0)
    def _():
        rows = arrived.shape[2]
        turned[...] = turn(arrived[...].reshape(half, rows))

    out[...] = dot(turned[...], table[0])


def restore_even(table, arrived):
    half = table.shape[1]
    devices, own, rows = arrived.shape
    tile = min(512, half)
    return pl.pallas_call(
        functools.partial(even_kernel, half=half),
        grid=(half // tile,),
        in_specs=[
            pl.BlockSpec((1, half, tile), lambda t: (0, 0, t)),
            pl.BlockSpec((devices, own, rows), lambda t: (0, 0, 0)),
        ],
        out_specs=pl.BlockSpec((rows, tile), lambda t: (0, t)),
        out_shape=jax.ShapeDtypeStruct((rows, half), jnp.float32),
        scratch_shapes=[pltpu.VMEM((rows, half), jnp.bfloat16)],
        compiler_params=pltpu.CompilerParams(vmem_limit_bytes=60 << 20),
        name="restore_even",
    )(table, arrived)


def odd_kernel(table, arrived, even, mirror, out, turned, *, half, tile):
    step = pl.program_id(0)

    @pl.when(step == 0)
    def _():
        rows = arrived.shape[2]
        turned[...] = turn(arrived[...].reshape(half, rows))

    odd = dot(turned[...], table[0])
    out[:, pl.ds(pl.multiple_of(step * tile, tile), tile)] = even[...] + odd
    left = even[...] - odd
    base = pl.multiple_of(2 * half - tile - step * tile, tile)
    for at in range(0, tile, lane_block):
        rest = left[:, at : at + lane_block]
        back = jnp.zeros_like(rest)
        for _ in range(3):
            piece = rest.astype(jnp.bfloat16)
            back += dot(piece, mirror[...])
            rest = rest - piece.astype(jnp.float32)
        out[:, pl.ds(base + tile - lane_block - at, lane_block)] = back


def restore(table, arrived, even, mirror):
    half = table.shape[1]
    devices, own, rows = arrived.shape
    tile = min(512, half)
    return pl.pallas_call(
        functools.partial(odd_kernel, half=half, tile=tile),
        grid=(half // tile,),
        in_specs=[
            pl.BlockSpec((1, half, tile), lambda t: (1, 0, t)),
            pl.BlockSpec((devices, own, rows), lambda t: (0, 0, 0)),
            pl.BlockSpec((rows, tile), lambda t: (0, t)),
            pl.BlockSpec((lane_block, lane_block), lambda t: (0, 0)),
        ],
        out_specs=pl.BlockSpec((rows, 2 * half), lambda t: (0, 0)),
        out_shape=jax.ShapeDtypeStruct((rows, 2 * half), jnp.float32),
        scratch_shapes=[pltpu.VMEM((rows, half), jnp.bfloat16)],
        compiler_params=pltpu.CompilerParams(vmem_limit_bytes=60 << 20),
        name="restore",
    )(table, arrived, even, mirror)


def body(slices, otf_rows, otf_cols):
    axes = ("focus", "strip")
    focus_count = lax.axis_size("focus")
    devices = focus_count * lax.axis_size("strip")
    rows, length = slices.shape[1:]
    half = length // 2
    piece = length // devices
    above, below = edge_rows(slices, 4)
    table = cosine_halves(length)
    weights = band()
    mirror = exchange_matrix()
    above, below, table = lax.optimization_barrier((above, below, table))
    head = jnp.pad(above, ((0, 0), (12, 0), (0, 0)))
    tail = jnp.pad(below, ((0, 0), (0, 12), (0, 0)))
    focus = lax.axis_index("focus")
    chunks = row_chunks if piece % (16 * row_chunks) == 0 else 1
    if piece // chunks * chunks != piece or piece < lane_block:
        chunks = 1
    chunk_rows = piece // chunks
    tile_rows = math.gcd(128, chunk_rows)
    swap = [(i, focus_count - 1 - i) for i in range(focus_count)]
    arrived = ([], [])
    for chunk in range(chunks):
        def sums(half_index):
            place = (half_index * piece + chunk * chunk_rows) // tile_rows
            return stencil(place.astype(jnp.int32).reshape(1), slices, head, tail, weights, chunk_rows)

        sent = sums(focus_count - 1 - focus)
        received = lax.ppermute(sent, "focus", swap)
        own = sums(focus)
        folded = merge(own, received, mirror)
        for parity in range(2):
            along = transform_rows(table, folded, parity, devices)
            moved = lax.all_to_all(along, axes, split_axis=0, concat_axis=0, tiled=True)
            arrived[parity].append(moved)
    blocks = length // lane_block
    per = lane_block // piece
    owner = focus * lax.axis_size("strip") + lax.axis_index("strip")
    own = half // devices
    rows_response = otf_rows.reshape(half, 2).T.reshape(2, 1, half)
    local_cols = lax.dynamic_slice_in_dim(otf_cols.reshape(half, 2), owner * own, own, 0)
    strips = devices // focus_count
    order = [b % focus_count * strips + b // focus_count if per == 1 else b for b in range(blocks)]
    restored = []
    for parity in range(2):
        parts = arrived[parity]
        if per > 1:
            parts = [
                part.reshape(focus_count, devices // focus_count, own, piece)
                .transpose(1, 0, 2, 3)
                .reshape(blocks, per, own, piece)
                .transpose(0, 2, 1, 3)
                .reshape(blocks, own, lane_block)
                for part in parts
            ]
        back = filter_columns(table, rows_response, local_cols[:, parity : parity + 1], mirror, parts, order)
        if per > 1:
            back = back.reshape(blocks, own, per, piece).transpose(0, 2, 1, 3).reshape(devices, own, piece)
        restored.append(lax.all_to_all(back, axes, split_axis=0, concat_axis=0, tiled=True))
    even = restore_even(table, restored[0])
    return restore(table, restored[1], even, mirror)


def solution(mesh):
    in_specs = (P(("field", "focus"), "strip", None), P(), P())
    out_specs = P(("field", "focus", "strip"), None)
    return jax.shard_map(body, mesh=mesh, in_specs=in_specs, out_specs=out_specs, check_vma=False)
```

```python
import functools
import math

import jax
import jax.numpy as jnp
from jax import lax
from jax.experimental import pallas as pl
from jax.experimental.pallas import tpu as pltpu
from jax.sharding import PartitionSpec as P


floor_weight = 0.01
noise_ratio = 0.01
lane_block = 256
row_chunks = 2


def dot(left, right):
    return jnp.dot(left, right, preferred_element_type=jnp.float32)


def dot_last(left, right):
    return lax.dot_general(left, right, (((1,), (1,)), ((), ())), preferred_element_type=jnp.float32)


def edge_rows(slices, width):
    count = lax.axis_size("strip")
    ends = count - 1
    head = slices[:, :width, :]
    tail = slices[:, slices.shape[1] - width :, :]
    above = lax.ppermute(tail, "strip", [(i, i + 1) for i in range(ends)])
    below = lax.ppermute(head, "strip", [(i + 1, i) for i in range(ends)])
    return above, below


def band():
    source = lax.broadcasted_iota(jnp.int32, (256, 512), 0)
    column = lax.broadcasted_iota(jnp.int32, (256, 512), 1)
    which = column // 128
    offset = source - column % 128 - 64
    spacing = jnp.where(which == 0, 1, jnp.where(which == 1, 2, 4))
    lap = jnp.where(offset == 0, -4.0, jnp.where(jnp.abs(offset) == spacing, 1.0, 0.0))
    return jnp.where(which == 3, jnp.where(offset == 0, 1.0, 0.0), lap).astype(jnp.bfloat16)


def exchange_matrix():
    row = lax.broadcasted_iota(jnp.int32, (lane_block, lane_block), 0)
    column = lax.broadcasted_iota(jnp.int32, (lane_block, lane_block), 1)
    return (row + column == lane_block - 1).astype(jnp.bfloat16)


def stencil_kernel(
    place, main, above, below, ends, weights, out,
    edges, copies_a, copies_b, laps_a, laps_b, held,
    *, tile_rows, count, cols, tiles, step, parts,
):
    tile = place[0] + pl.program_id(0)
    first = tile == 0
    last = tile == tiles - 1
    edge_row = lax.broadcasted_iota(jnp.int32, (16, cols), 0)
    lane = lax.broadcasted_iota(jnp.int32, (step, 128), 1)
    for s in range(count):
        upper = jnp.where(first, ends[s], above[s])
        lower = jnp.where(last, ends[s], below[s])
        edges[s] = jnp.where(edge_row < 8, lower, upper)
    frames = cols // 128 + 1
    copies = (copies_a, copies_b)
    laps = (laps_a, laps_b)

    def start_of(frame):
        return frame * 128 - 128 if isinstance(frame, int) else pl.multiple_of(frame * 128 - 128, 128)

    def window(source, frame, rows, low, high):
        size = (high - low) * rows
        if isinstance(frame, int) and frame == 0:
            piece = source[low:high, :, pl.ds(0, 128)].reshape(size, 128)
            return jnp.concatenate([jnp.zeros_like(piece), piece], axis=1)
        if isinstance(frame, int) and frame == frames - 1:
            piece = source[low:high, :, pl.ds(cols - 128, 128)].reshape(size, 128)
            return jnp.concatenate([piece, jnp.zeros_like(piece)], axis=1)
        return source[low:high, :, pl.ds(start_of(frame), 256)].reshape(size, 256)

    def spread_edges(slot, frame):
        rows = dot(window(edges, frame, 16, 0, count), weights[:, pl.ds(384, 128)])
        for s in range(count):
            copies[slot][s, pl.ds(0, 8), :] = rows[16 * s + 8 : 16 * s + 16]
            copies[slot][s, pl.ds(8 + tile_rows, 8), :] = rows[16 * s : 16 * s + 8]

    def spread(slot, frame, low, high):
        rows = dot(window(main, frame, tile_rows, low, high), weights[...])
        for s in range(low, high):
            at = (s - low) * tile_rows
            copies[slot][s, pl.ds(8, tile_rows), :] = rows[at : at + tile_rows, 384:]
            for k in range(3):
                laps[slot][s, k] = rows[at : at + tile_rows, 128 * k : 128 * k + 128]

    def gather(slot, frame, low, high):
        for r in range(low, high, step):
            numerator = jnp.zeros((step, 128), jnp.float32)
            denominator = numerator
            for s in range(count):
                centers = copies[slot]

                def lap(k, d):
                    pair = centers[s, pl.ds(8 + r + d, step), :] + centers[s, pl.ds(8 + r - d, step), :]
                    return laps[slot][s, k, pl.ds(r, step), :] + pair

                fine, middle, coarse = lap(0, 1), lap(1, 2), lap(2, 4)
                weight = floor_weight + (
                    fine * fine + 0.5 * (middle * middle + 0.5 * (coarse * coarse))
                )
                numerator += weight * centers[s, pl.ds(8 + r, step), :]
                denominator += weight
            for k, value in enumerate((numerator, denominator)):
                turned = pltpu.roll(value, 64, 1)
                if not (isinstance(frame, int) and frame == 0):
                    joined = jnp.where(lane < 64, held[k, pl.ds(r, step), :], turned)
                    out[k, pl.ds(r, step), pl.ds(start_of(frame), 128)] = joined
                held[k, pl.ds(r, step), :] = turned

    def both(slot, frame):
        spread_edges(slot, frame)
        for q in range(parts):
            spread(slot, frame, q * count // parts, (q + 1) * count // parts)
            gather(1 - slot, frame - 1, q * tile_rows // parts, (q + 1) * tile_rows // parts)

    spread_edges(0, 0)
    spread(0, 0, 0, count)
    both(1, 1)
    both(0, 2)

    def two(i, carry):
        both(1, 2 * i + 1)
        both(0, 2 * i + 2)
        return carry

    lax.fori_loop(1, frames // 2 - 1, two, 0)
    both(1, frames - 2)
    both(0, frames - 1)
    gather(0, frames - 1, 0, tile_rows)


def stencil(place, slices, ends, weights, out_rows):
    count, rows, cols = slices.shape
    tile_rows = math.gcd(128, out_rows)
    per = tile_rows // 16
    blocks = rows // 16
    step = min(16, tile_rows)
    parts = math.gcd(math.gcd(4, count), tile_rows // step)
    kernel = functools.partial(
        stencil_kernel, tile_rows=tile_rows, count=count, cols=cols, tiles=rows // tile_rows, step=step, parts=parts
    )
    edge = (count, 16, cols)
    grid_spec = pltpu.PrefetchScalarGridSpec(
        num_scalar_prefetch=1,
        grid=(out_rows // tile_rows,),
        in_specs=[
            pl.BlockSpec((count, tile_rows, cols), lambda t, at: (0, at[0] + t, 0)),
            pl.BlockSpec(edge, lambda t, at: (0, jnp.maximum((at[0] + t) * per - 1, 0), 0)),
            pl.BlockSpec(edge, lambda t, at: (0, jnp.minimum((at[0] + t) * per + per, blocks - 1), 0)),
            pl.BlockSpec(edge, lambda t, at: (0, 0, 0)),
            pl.BlockSpec((256, 512), lambda t, at: (0, 0)),
        ],
        out_specs=pl.BlockSpec((2, tile_rows, cols), lambda t, at: (0, t, 0)),
        scratch_shapes=[
            pltpu.VMEM(edge, jnp.bfloat16),
            pltpu.VMEM((count, tile_rows + 16, 128), jnp.float32),
            pltpu.VMEM((count, tile_rows + 16, 128), jnp.float32),
            pltpu.VMEM((count, 3, tile_rows, 128), jnp.float32),
            pltpu.VMEM((count, 3, tile_rows, 128), jnp.float32),
            pltpu.VMEM((2, tile_rows, 128), jnp.float32),
        ],
    )
    pixels = count * out_rows * cols
    return pl.pallas_call(
        kernel,
        grid_spec=grid_spec,
        out_shape=jax.ShapeDtypeStruct((2, out_rows, cols), jnp.float32),
        cost_estimate=pl.CostEstimate(flops=pixels * 2048, bytes_accessed=pixels * 3, transcendentals=0),
        compiler_params=pltpu.CompilerParams(vmem_limit_bytes=60 << 20),
        name="stencil",
    )(place, slices, slices, slices, ends, weights)


def table_kernel(near, turn, out, *, half):
    parity, block = pl.program_id(0), pl.program_id(1)
    group = min(64, out.shape[1])
    norm = math.sqrt(1.0 / half)
    for at in range(0, out.shape[1], group):
        rows = pl.ds(at, group)
        near_cos, near_sin, step_cos, step_sin = (near[0, k, rows, :] for k in range(4))
        low_cos = near_cos * turn[0, 0] - near_sin * turn[0, 1]
        low_sin = near_sin * turn[0, 0] + near_cos * turn[0, 1]
        row = at + lax.broadcasted_iota(jnp.int32, low_cos.shape, 0)
        first = (row == 0) & (parity == 0) & (block == 0)
        scale = jnp.where(first, norm * math.sqrt(0.5), norm)
        before = scale * low_cos
        here = scale * (step_cos * low_cos - step_sin * low_sin)
        twice = step_cos + step_cos
        out[0, rows, pl.ds(0, 128)] = before.astype(jnp.bfloat16)
        for j in range(1, half // 128):
            out[0, rows, pl.ds(j * 128, 128)] = here.astype(jnp.bfloat16)
            before, here = here, twice * here - before


def cosine_halves(length):
    half = length // 2
    rows = min(256, half)
    assert 512 * rows % (4 * length) == 0
    unit = jnp.float32(math.pi / (2 * length))

    def pair(phase):
        angle = (phase % (4 * length)).astype(jnp.float32) * unit
        return [jnp.cos(angle), jnp.sin(angle)]

    def iota(shape, dim):
        return lax.broadcasted_iota(jnp.int32, shape, dim)

    odd = (2, rows, 128)
    frequency = 2 * iota(odd, 1) + iota(odd, 0)
    near = jnp.stack(pair((2 * iota(odd, 2) + 1) * frequency) + pair(256 * frequency), axis=1)
    blocks = (half // rows, 1, 128)
    turn = jnp.stack(pair((2 * iota(blocks, 2) + 1) * (2 * rows * iota(blocks, 0))), axis=1)
    return pl.pallas_call(
        functools.partial(table_kernel, half=half),
        grid=(2, half // rows),
        in_specs=[
            pl.BlockSpec((1, 4, rows, 128), lambda p, b: (p, 0, 0, 0)),
            pl.BlockSpec((1, 2, 1, 128), lambda p, b: (b, 0, 0, 0)),
        ],
        out_specs=pl.BlockSpec((1, rows, half), lambda p, b: (p, b, 0)),
        out_shape=jax.ShapeDtypeStruct((2, half, half), jnp.bfloat16),
        name="cosines",
    )(near, turn)


def merge_kernel(own, other, mirror, out, *, cols):
    def merged(at):
        numerator = own[0, :, pl.ds(at, lane_block)] + other[0, :, pl.ds(at, lane_block)]
        denominator = own[1, :, pl.ds(at, lane_block)] + other[1, :, pl.ds(at, lane_block)]
        return (numerator / denominator).astype(jnp.bfloat16)

    for at in range(0, cols // 2, lane_block):
        near = merged(at).astype(jnp.float32)
        far = dot(merged(cols - lane_block - at), mirror[...])
        out[0, :, pl.ds(at, lane_block)] = (near + far).astype(jnp.bfloat16)
        out[1, :, pl.ds(at, lane_block)] = (near - far).astype(jnp.bfloat16)


def merge(own, other, mirror, at):
    _, rows, cols = own.shape
    tile = min(64, rows)
    first = at // tile
    return pl.pallas_call(
        functools.partial(merge_kernel, cols=cols),
        grid=(rows // tile,),
        in_specs=[
            pl.BlockSpec((2, tile, cols), lambda t: (0, t, 0)),
            pl.BlockSpec((2, tile, cols), lambda t: (0, first + t, 0)),
            pl.BlockSpec((lane_block, lane_block), lambda t: (0, 0)),
        ],
        out_specs=pl.BlockSpec((2, tile, cols // 2), lambda t: (0, t, 0)),
        out_shape=jax.ShapeDtypeStruct((2, rows, cols // 2), jnp.bfloat16),
        name="merge",
    )(own, other, mirror)


def rows_kernel(table, folded, out):
    values = dot_last(table[0], folded[0]).astype(jnp.bfloat16)
    out[...] = values.reshape(out.shape)


def transform_rows(table, folded, parities, devices):
    _, rows, half = folded.shape
    own = half // devices
    tile = max(512, own)
    first = parities[0]
    return pl.pallas_call(
        rows_kernel,
        grid=(len(parities), half // tile),
        in_specs=[
            pl.BlockSpec((1, tile, half), lambda p, t: (first + p, t, 0)),
            pl.BlockSpec((1, rows, half), lambda p, t: (first + p, 0, 0)),
        ],
        out_specs=pl.BlockSpec((tile // own, 1, own, rows), lambda p, t: (t, p, 0, 0)),
        out_shape=jax.ShapeDtypeStruct((devices, len(parities), own, rows), jnp.bfloat16),
        name="transform_rows",
    )(table, folded)


def columns_kernel(*refs, chunks, half, order):
    table, rows_response, cols_response, mirror = refs[:4]
    arrived = refs[4 : 4 + chunks]
    out, folded, total = refs[4 + chunks :]
    parity = pl.program_id(0)
    step = pl.program_id(1)
    blocks = half // lane_block

    @pl.when((parity == 0) & (step == 0))
    def _():
        for j in range(blocks):
            near = jnp.concatenate([part[order[j], 0] for part in arrived], axis=1).astype(jnp.float32)
            far = dot(
                jnp.concatenate([part[order[2 * blocks - 1 - j], 0] for part in arrived], axis=1), mirror[...]
            )
            folded[0, :, pl.ds(j * lane_block, lane_block)] = (near + far).astype(jnp.bfloat16)
            folded[1, :, pl.ds(j * lane_block, lane_block)] = (near - far).astype(jnp.bfloat16)

    spectrum = dot_last(folded[parity], table[0])
    response = cols_response[...] * rows_response[0]
    filtered = (spectrum * (response / (response * response + noise_ratio))).astype(jnp.bfloat16)
    part = dot(filtered, table[0])

    @pl.when(step == 0)
    def _():
        total[parity] = part

    @pl.when(step > 0)
    def _():
        total[parity] += part

    @pl.when((parity == 1) & (step == pl.num_programs(1) - 1))
    def _():
        for j in range(blocks):
            even = total[0, :, pl.ds(j * lane_block, lane_block)]
            odd = total[1, :, pl.ds(j * lane_block, lane_block)]
            out[j] = (even + odd).astype(jnp.bfloat16)
            out[2 * blocks - 1 - j] = dot((even - odd).astype(jnp.bfloat16), mirror[...]).astype(jnp.bfloat16)


def filter_columns(table, rows_response, cols_response, mirror, arrived, order):
    half = table.shape[1]
    blocks, _, own, _ = arrived[0][0].shape
    tile = min(512, half)
    chunks = len(arrived)

    def whole(part, parity):
        return pl.BlockSpec((blocks, 1, own, part.shape[3]), lambda p, t: (0, parity, 0, 0))

    return pl.pallas_call(
        functools.partial(columns_kernel, chunks=chunks, half=half, order=order),
        grid=(2, half // tile),
        in_specs=[
            pl.BlockSpec((1, tile, half), lambda p, t: (p, t, 0)),
            pl.BlockSpec((1, 1, tile), lambda p, t: (p, 0, t)),
            pl.BlockSpec((own, 1), lambda p, t: (0, 0)),
            pl.BlockSpec((lane_block, lane_block), lambda p, t: (0, 0)),
        ]
        + [whole(*pair) for pair in arrived],
        out_specs=pl.BlockSpec((blocks, own, lane_block), lambda p, t: (0, 0, 0)),
        out_shape=jax.ShapeDtypeStruct((blocks, own, lane_block), jnp.bfloat16),
        scratch_shapes=[
            pltpu.VMEM((2, own, half), jnp.bfloat16),
            pltpu.VMEM((2, own, half), jnp.float32),
        ],
        compiler_params=pltpu.CompilerParams(vmem_limit_bytes=60 << 20),
        name="filter_columns",
    )(table, rows_response, cols_response, mirror, *(part for part, _ in arrived))


def turn(values):
    return jnp.transpose(values.astype(jnp.float32)).astype(jnp.bfloat16)


def even_kernel(table, arrived, out, turned, *, half):
    @pl.when(pl.program_id(0) == 0)
    def _():
        rows = arrived.shape[2]
        turned[...] = turn(arrived[...].reshape(half, rows))

    out[...] = dot(turned[...], table[0])


def restore_even(table, arrived):
    half = table.shape[1]
    devices, own, rows = arrived.shape
    tile = min(512, half)
    return pl.pallas_call(
        functools.partial(even_kernel, half=half),
        grid=(half // tile,),
        in_specs=[
            pl.BlockSpec((1, half, tile), lambda t: (0, 0, t)),
            pl.BlockSpec((devices, own, rows), lambda t: (0, 0, 0)),
        ],
        out_specs=pl.BlockSpec((rows, tile), lambda t: (0, t)),
        out_shape=jax.ShapeDtypeStruct((rows, half), jnp.float32),
        scratch_shapes=[pltpu.VMEM((rows, half), jnp.bfloat16)],
        compiler_params=pltpu.CompilerParams(vmem_limit_bytes=60 << 20),
        name="restore_even",
    )(table, arrived)


def odd_kernel(table, arrived, even, mirror, out, turned, *, half, tile):
    step = pl.program_id(0)

    @pl.when(step == 0)
    def _():
        rows = arrived.shape[2]
        turned[...] = turn(arrived[...].reshape(half, rows))

    odd = dot(turned[...], table[0])
    out[:, pl.ds(pl.multiple_of(step * tile, tile), tile)] = even[...] + odd
    left = even[...] - odd
    base = pl.multiple_of(2 * half - tile - step * tile, tile)
    for at in range(0, tile, lane_block):
        rest = left[:, at : at + lane_block]
        back = jnp.zeros_like(rest)
        for _ in range(3):
            piece = rest.astype(jnp.bfloat16)
            back += dot(piece, mirror[...])
            rest = rest - piece.astype(jnp.float32)
        out[:, pl.ds(base + tile - lane_block - at, lane_block)] = back


def restore(table, arrived, even, mirror):
    half = table.shape[1]
    devices, own, rows = arrived.shape
    tile = min(512, half)
    return pl.pallas_call(
        functools.partial(odd_kernel, half=half, tile=tile),
        grid=(half // tile,),
        in_specs=[
            pl.BlockSpec((1, half, tile), lambda t: (1, 0, t)),
            pl.BlockSpec((devices, own, rows), lambda t: (0, 0, 0)),
            pl.BlockSpec((rows, tile), lambda t: (0, t)),
            pl.BlockSpec((lane_block, lane_block), lambda t: (0, 0)),
        ],
        out_specs=pl.BlockSpec((rows, 2 * half), lambda t: (0, 0)),
        out_shape=jax.ShapeDtypeStruct((rows, 2 * half), jnp.float32),
        scratch_shapes=[pltpu.VMEM((rows, half), jnp.bfloat16)],
        compiler_params=pltpu.CompilerParams(vmem_limit_bytes=60 << 20),
        name="restore",
    )(table, arrived, even, mirror)


def program(slices, otf_rows, otf_cols):
    axes = ("focus", "strip")
    focus_count = lax.axis_size("focus")
    devices = focus_count * lax.axis_size("strip")
    _, length = slices.shape[1:]
    half = length // 2
    piece = length // devices
    blocks = length // lane_block
    per = lane_block // piece
    above, below = edge_rows(slices, 4)
    table = cosine_halves(length)
    weights = band()
    mirror = exchange_matrix()
    focus = lax.axis_index("focus")
    owner = focus * lax.axis_size("strip") + lax.axis_index("strip")
    own = half // devices
    rows_response = otf_rows.reshape(half, 2).T.reshape(2, 1, half)
    local_cols = lax.dynamic_slice_in_dim(otf_cols, owner * 2 * own, 2 * own, 0).reshape(own, 2).T.reshape(2, own, 1)
    above, below, table, rows_response, local_cols, mirror, weights = lax.optimization_barrier(
        (above, below, table, rows_response, local_cols, mirror, weights)
    )
    ends = jnp.pad(above, ((0, 0), (12, 0), (0, 0))) + jnp.pad(below, ((0, 0), (0, 12), (0, 0)))
    chunks = row_chunks if per == 1 and piece % (16 * row_chunks) == 0 else 1
    chunk_rows = piece // chunks
    swap = [(i, focus_count - 1 - i) for i in range(focus_count)]

    def sums(ends, half_index, chunk, rows):
        place = (half_index * piece + chunk * chunk_rows) // math.gcd(128, rows)
        return stencil(place.astype(jnp.int32).reshape(1), slices, ends, weights, rows)

    last = []

    def exchange(values):
        if last:
            values, _ = lax.optimization_barrier((values, last[-1]))
        last.append(lax.all_to_all(values, axes, split_axis=0, concat_axis=0, tiled=True))
        return last[-1]

    received = lax.ppermute(sums(ends, focus_count - 1 - focus, 0, piece), "focus", swap)
    arrived = ([], [])
    for chunk in range(chunks):
        own_sums = sums(ends, focus, chunk, chunk_rows)
        folded = merge(own_sums, received, mirror, chunk * chunk_rows)
        for parities in ((0,), (1,)) if chunk == chunks - 1 else ((0, 1),):
            along = transform_rows(table, folded, parities, devices)
            if chunk < chunks - 1:
                ends, along = lax.optimization_barrier((ends, along))
            moved = exchange(along)
            for at, parity in enumerate(parities):
                arrived[parity].append((moved, at))
    strips = devices // focus_count
    order = [b % focus_count * strips + b // focus_count if per == 1 else b for b in range(blocks)]
    restored = []
    for parity in range(2):
        parts = arrived[parity]
        if per > 1:
            parts = [
                (
                    part.reshape(focus_count, devices // focus_count, own, piece)
                    .transpose(1, 0, 2, 3)
                    .reshape(blocks, per, own, piece)
                    .transpose(0, 2, 1, 3)
                    .reshape(blocks, 1, own, lane_block),
                    0,
                )
                for part, _ in parts
            ]
        back = filter_columns(table, rows_response, local_cols[parity], mirror, parts, order)
        if per > 1:
            back = back.reshape(blocks, own, per, piece).transpose(0, 2, 1, 3).reshape(devices, own, piece)
        restored.append(exchange(back))
    even = restore_even(table, restored[0])
    return restore(table, restored[1], even, mirror)


def solution(mesh):
    in_specs = (P(("field", "focus"), "strip", None), P(), P())
    out_specs = P(("field", "focus", "strip"), None)
    return jax.shard_map(program, mesh=mesh, in_specs=in_specs, out_specs=out_specs, check_vma=False)
```

```python
import functools
import math

import jax
import jax.numpy as jnp
from jax import lax
from jax.experimental import pallas as pl
from jax.experimental.pallas import tpu as pltpu
from jax.sharding import PartitionSpec as P


floor_weight = 0.01
noise_ratio = 0.01
lane_block = 256
row_chunks = 2


def dot(left, right):
    return jnp.dot(left, right, preferred_element_type=jnp.float32)


def dot_last(left, right):
    return lax.dot_general(left, right, (((1,), (1,)), ((), ())), preferred_element_type=jnp.float32)


def edge_rows(slices, width):
    count = lax.axis_size("strip")
    ends = count - 1
    head = slices[:, :width, :]
    tail = slices[:, slices.shape[1] - width :, :]
    above = lax.ppermute(tail, "strip", [(i, i + 1) for i in range(ends)])
    below = lax.ppermute(head, "strip", [(i + 1, i) for i in range(ends)])
    return above, below


def band():
    source = lax.broadcasted_iota(jnp.int32, (256, 512), 0)
    column = lax.broadcasted_iota(jnp.int32, (256, 512), 1)
    which = column // 128
    offset = source - column % 128 - 64
    spacing = jnp.where(which == 0, 1, jnp.where(which == 1, 2, 4))
    lap = jnp.where(offset == 0, -4.0, jnp.where(jnp.abs(offset) == spacing, 1.0, 0.0))
    return jnp.where(which == 3, jnp.where(offset == 0, 1.0, 0.0), lap).astype(jnp.bfloat16)


def exchange_matrix():
    row = lax.broadcasted_iota(jnp.int32, (lane_block, lane_block), 0)
    column = lax.broadcasted_iota(jnp.int32, (lane_block, lane_block), 1)
    return (row + column == lane_block - 1).astype(jnp.bfloat16)


def stencil_kernel(
    place, main, above, below, ends, weights, out,
    edges, copies_a, copies_b, laps_a, laps_b, joined,
    *, tile_rows, count, cols, tiles, step, parts,
):
    tile = place[0] + pl.program_id(0)
    first = tile == 0
    last = tile == tiles - 1
    edge_row = lax.broadcasted_iota(jnp.int32, (16, cols), 0)
    for s in range(count):
        upper = jnp.where(first, ends[s], above[s])
        lower = jnp.where(last, ends[s], below[s])
        edges[s] = jnp.where(edge_row < 8, lower, upper)
    frames = cols // 128 + 1
    copies = (copies_a, copies_b)
    laps = (laps_a, laps_b)

    def start_of(frame):
        return frame * 128 - 128 if isinstance(frame, int) else pl.multiple_of(frame * 128 - 128, 128)

    def window(source, frame, rows, low, high):
        size = (high - low) * rows
        if isinstance(frame, int) and frame == 0:
            piece = source[low:high, :, pl.ds(0, 128)].reshape(size, 128)
            return jnp.concatenate([jnp.zeros_like(piece), piece], axis=1)
        if isinstance(frame, int) and frame == frames - 1:
            piece = source[low:high, :, pl.ds(cols - 128, 128)].reshape(size, 128)
            return jnp.concatenate([piece, jnp.zeros_like(piece)], axis=1)
        return source[low:high, :, pl.ds(start_of(frame), 256)].reshape(size, 256)

    def spread_edges(slot, frame):
        rows = dot(window(edges, frame, 16, 0, count), weights[:, pl.ds(384, 128)])
        for s in range(count):
            copies[slot][s, pl.ds(0, 8), :] = rows[16 * s + 8 : 16 * s + 16]
            copies[slot][s, pl.ds(8 + tile_rows, 8), :] = rows[16 * s : 16 * s + 8]

    def spread(slot, frame, low, high):
        rows = dot(window(main, frame, tile_rows, low, high), weights[...])
        for s in range(low, high):
            at = (s - low) * tile_rows
            copies[slot][s, pl.ds(8, tile_rows), :] = rows[at : at + tile_rows, 384:]
            for k in range(3):
                laps[slot][s, k] = rows[at : at + tile_rows, 128 * k : 128 * k + 128]

    def gather(slot, frame, low, high):
        for r in range(low, high, step):
            numerator = jnp.zeros((step, 128), jnp.float32)
            denominator = numerator
            for s in range(count):
                centers = copies[slot]

                def lap(k, d):
                    pair = centers[s, pl.ds(8 + r + d, step), :] + centers[s, pl.ds(8 + r - d, step), :]
                    return laps[slot][s, k, pl.ds(r, step), :] + pair

                fine, middle, coarse = lap(0, 1), lap(1, 2), lap(2, 4)
                weight = floor_weight + (
                    fine * fine + 0.5 * (middle * middle + 0.5 * (coarse * coarse))
                )
                numerator += weight * centers[s, pl.ds(8 + r, step), :]
                denominator += weight
            joined[0, frame, pl.ds(r, step), :] = numerator
            joined[1, frame, pl.ds(r, step), :] = denominator

    def both(slot, frame):
        spread_edges(slot, frame)
        for q in range(parts):
            spread(slot, frame, q * count // parts, (q + 1) * count // parts)
            gather(1 - slot, frame - 1, q * tile_rows // parts, (q + 1) * tile_rows // parts)

    spread_edges(0, 0)
    spread(0, 0, 0, count)
    both(1, 1)
    both(0, 2)

    def two(i, carry):
        both(1, 2 * i + 1)
        both(0, 2 * i + 2)
        return carry

    lax.fori_loop(1, frames // 2 - 1, two, 0)
    both(1, frames - 2)
    both(0, frames - 1)
    gather(0, frames - 1, 0, tile_rows)
    lane = lax.broadcasted_iota(jnp.int32, (tile_rows, 128), 1)

    def shift_back(j, carry):
        at = pl.ds(pl.multiple_of(j * 128, 128), 128)
        for k in range(2):
            out[k, :, at] = pltpu.roll(jnp.where(lane >= 64, joined[k, j], joined[k, j + 1]), 64, 1)
        return carry

    lax.fori_loop(0, frames - 1, shift_back, 0)


def stencil(place, slices, ends, weights, out_rows):
    count, rows, cols = slices.shape
    tile_rows = math.gcd(128, out_rows)
    per = tile_rows // 16
    blocks = rows // 16
    step = min(16, tile_rows)
    parts = 1
    kernel = functools.partial(
        stencil_kernel, tile_rows=tile_rows, count=count, cols=cols, tiles=rows // tile_rows, step=step, parts=parts
    )
    edge = (count, 16, cols)
    grid_spec = pltpu.PrefetchScalarGridSpec(
        num_scalar_prefetch=1,
        grid=(out_rows // tile_rows,),
        in_specs=[
            pl.BlockSpec((count, tile_rows, cols), lambda t, at: (0, at[0] + t, 0)),
            pl.BlockSpec(edge, lambda t, at: (0, jnp.maximum((at[0] + t) * per - 1, 0), 0)),
            pl.BlockSpec(edge, lambda t, at: (0, jnp.minimum((at[0] + t) * per + per, blocks - 1), 0)),
            pl.BlockSpec(edge, lambda t, at: (0, 0, 0)),
            pl.BlockSpec((256, 512), lambda t, at: (0, 0)),
        ],
        out_specs=pl.BlockSpec((2, tile_rows, cols), lambda t, at: (0, t, 0)),
        scratch_shapes=[
            pltpu.VMEM(edge, jnp.bfloat16),
            pltpu.VMEM((count, tile_rows + 16, 128), jnp.float32),
            pltpu.VMEM((count, tile_rows + 16, 128), jnp.float32),
            pltpu.VMEM((count, 3, tile_rows, 128), jnp.float32),
            pltpu.VMEM((count, 3, tile_rows, 128), jnp.float32),
            pltpu.VMEM((2, cols // 128 + 1, tile_rows, 128), jnp.float32),
        ],
    )
    pixels = count * out_rows * cols
    return pl.pallas_call(
        kernel,
        grid_spec=grid_spec,
        out_shape=jax.ShapeDtypeStruct((2, out_rows, cols), jnp.float32),
        cost_estimate=pl.CostEstimate(flops=pixels * 2048, bytes_accessed=pixels * 3, transcendentals=0),
        compiler_params=pltpu.CompilerParams(vmem_limit_bytes=60 << 20),
        name="stencil",
    )(place, slices, slices, slices, ends, weights)


def table_kernel(near, turn, out, *, half):
    parity, block = pl.program_id(0), pl.program_id(1)
    period = near.shape[2]
    group = min(64, period)
    norm = math.sqrt(1.0 / half)

    def fill(b, carry):
        for at in range(0, period, group):
            near_cos, near_sin, step_cos, step_sin = (near[0, k, pl.ds(at, group), :] for k in range(4))
            low_cos = near_cos * turn[b, 0] - near_sin * turn[b, 1]
            low_sin = near_sin * turn[b, 0] + near_cos * turn[b, 1]
            row = at + lax.broadcasted_iota(jnp.int32, low_cos.shape, 0)
            first = (row == 0) & (parity == 0) & (block == 0) & (b == 0)
            scale = jnp.where(first, norm * math.sqrt(0.5), norm)
            before = scale * low_cos
            here = scale * (step_cos * low_cos - step_sin * low_sin)
            twice = step_cos + step_cos
            rows = pl.ds(pl.multiple_of(b * period + at, group), group)
            out[0, rows, pl.ds(0, 128)] = before.astype(jnp.bfloat16)
            for j in range(1, half // 128):
                out[0, rows, pl.ds(j * 128, 128)] = here.astype(jnp.bfloat16)
                before, here = here, twice * here - before
        return carry

    lax.fori_loop(0, out.shape[1] // period, fill, 0)


def cosine_halves(length):
    half = length // 2
    rows = min(256, half)
    tall = min(1024, half)
    assert 512 * rows % (4 * length) == 0
    unit = jnp.float32(math.pi / (2 * length))

    def pair(phase):
        angle = (phase % (4 * length)).astype(jnp.float32) * unit
        return [jnp.cos(angle), jnp.sin(angle)]

    def iota(shape, dim):
        return lax.broadcasted_iota(jnp.int32, shape, dim)

    odd = (2, rows, 128)
    frequency = 2 * iota(odd, 1) + iota(odd, 0)
    near = jnp.stack(pair((2 * iota(odd, 2) + 1) * frequency) + pair(256 * frequency), axis=1)
    blocks = (half // rows, 1, 128)
    turn = jnp.stack(pair((2 * iota(blocks, 2) + 1) * (2 * rows * iota(blocks, 0))), axis=1)
    return pl.pallas_call(
        functools.partial(table_kernel, half=half),
        grid=(2, half // tall),
        in_specs=[
            pl.BlockSpec((1, 4, rows, 128), lambda p, b: (p, 0, 0, 0)),
            pl.BlockSpec((tall // rows, 2, 1, 128), lambda p, b: (b, 0, 0, 0)),
        ],
        out_specs=pl.BlockSpec((1, tall, half), lambda p, b: (p, b, 0)),
        out_shape=jax.ShapeDtypeStruct((2, half, half), jnp.bfloat16),
        name="cosines",
    )(near, turn)


def merge_kernel(own, other, mirror, out, *, cols):
    def merged(at):
        numerator = own[0, :, pl.ds(at, lane_block)] + other[0, :, pl.ds(at, lane_block)]
        denominator = own[1, :, pl.ds(at, lane_block)] + other[1, :, pl.ds(at, lane_block)]
        return (numerator / denominator).astype(jnp.bfloat16)

    for at in range(0, cols // 2, lane_block):
        near = merged(at).astype(jnp.float32)
        far = dot(merged(cols - lane_block - at), mirror[...])
        out[0, :, pl.ds(at, lane_block)] = (near + far).astype(jnp.bfloat16)
        out[1, :, pl.ds(at, lane_block)] = (near - far).astype(jnp.bfloat16)


def merge(own, other, mirror, at):
    _, rows, cols = own.shape
    tile = min(64, rows)
    first = at // tile
    return pl.pallas_call(
        functools.partial(merge_kernel, cols=cols),
        grid=(rows // tile,),
        in_specs=[
            pl.BlockSpec((2, tile, cols), lambda t: (0, t, 0)),
            pl.BlockSpec((2, tile, cols), lambda t: (0, first + t, 0)),
            pl.BlockSpec((lane_block, lane_block), lambda t: (0, 0)),
        ],
        out_specs=pl.BlockSpec((2, tile, cols // 2), lambda t: (0, t, 0)),
        out_shape=jax.ShapeDtypeStruct((2, rows, cols // 2), jnp.bfloat16),
        name="merge",
    )(own, other, mirror)


def rows_kernel(table, folded, out):
    values = dot_last(table[0], folded[0]).astype(jnp.bfloat16)
    out[...] = values.reshape(out.shape)


def transform_rows(table, folded, parities, devices):
    _, rows, half = folded.shape
    own = half // devices
    tile = max(1024, own)
    first = parities[0]
    return pl.pallas_call(
        rows_kernel,
        grid=(len(parities), half // tile),
        in_specs=[
            pl.BlockSpec((1, tile, half), lambda p, t: (first + p, t, 0)),
            pl.BlockSpec((1, rows, half), lambda p, t: (first + p, 0, 0)),
        ],
        out_specs=pl.BlockSpec((tile // own, 1, own, rows), lambda p, t: (t, p, 0, 0)),
        out_shape=jax.ShapeDtypeStruct((devices, len(parities), own, rows), jnp.bfloat16),
        name="transform_rows",
    )(table, folded)


def columns_kernel(*refs, chunks, half, order):
    table, rows_response, cols_response, mirror = refs[:4]
    arrived = refs[4 : 4 + chunks]
    out, folded, total = refs[4 + chunks :]
    parity = pl.program_id(0)
    step = pl.program_id(1)
    blocks = half // lane_block

    @pl.when((parity == 0) & (step == 0))
    def _():
        for j in range(blocks):
            near = jnp.concatenate([part[order[j], 0] for part in arrived], axis=1).astype(jnp.float32)
            far = dot(
                jnp.concatenate([part[order[2 * blocks - 1 - j], 0] for part in arrived], axis=1), mirror[...]
            )
            folded[0, :, pl.ds(j * lane_block, lane_block)] = (near + far).astype(jnp.bfloat16)
            folded[1, :, pl.ds(j * lane_block, lane_block)] = (near - far).astype(jnp.bfloat16)

    spectrum = dot_last(folded[parity], table[0])
    response = cols_response[...] * rows_response[0]
    filtered = (spectrum * (response / (response * response + noise_ratio))).astype(jnp.bfloat16)
    part = dot(filtered, table[0])

    @pl.when(step == 0)
    def _():
        total[parity] = part

    @pl.when(step > 0)
    def _():
        total[parity] += part

    @pl.when((parity == 1) & (step == pl.num_programs(1) - 1))
    def _():
        for j in range(blocks):
            even = total[0, :, pl.ds(j * lane_block, lane_block)]
            odd = total[1, :, pl.ds(j * lane_block, lane_block)]
            out[j] = (even + odd).astype(jnp.bfloat16)
            out[2 * blocks - 1 - j] = dot((even - odd).astype(jnp.bfloat16), mirror[...]).astype(jnp.bfloat16)


def filter_columns(table, rows_response, cols_response, mirror, arrived, order):
    half = table.shape[1]
    blocks, _, own, _ = arrived[0][0].shape
    tile = min(1024, half)
    chunks = len(arrived)

    def whole(part, parity):
        return pl.BlockSpec((blocks, 1, own, part.shape[3]), lambda p, t: (0, parity, 0, 0))

    return pl.pallas_call(
        functools.partial(columns_kernel, chunks=chunks, half=half, order=order),
        grid=(2, half // tile),
        in_specs=[
            pl.BlockSpec((1, tile, half), lambda p, t: (p, t, 0)),
            pl.BlockSpec((1, 1, tile), lambda p, t: (p, 0, t)),
            pl.BlockSpec((own, 1), lambda p, t: (0, 0)),
            pl.BlockSpec((lane_block, lane_block), lambda p, t: (0, 0)),
        ]
        + [whole(*pair) for pair in arrived],
        out_specs=pl.BlockSpec((blocks, own, lane_block), lambda p, t: (0, 0, 0)),
        out_shape=jax.ShapeDtypeStruct((blocks, own, lane_block), jnp.bfloat16),
        scratch_shapes=[
            pltpu.VMEM((2, own, half), jnp.bfloat16),
            pltpu.VMEM((2, own, half), jnp.float32),
        ],
        compiler_params=pltpu.CompilerParams(vmem_limit_bytes=60 << 20),
        name="filter_columns",
    )(table, rows_response, cols_response, mirror, *(part for part, _ in arrived))


def turn(values):
    return jnp.transpose(values.astype(jnp.float32)).astype(jnp.bfloat16)


def even_kernel(table, arrived, out, turned, *, half):
    @pl.when(pl.program_id(0) == 0)
    def _():
        rows = arrived.shape[2]
        turned[...] = turn(arrived[...].reshape(half, rows))

    out[...] = dot(turned[...], table[0])


def restore_even(table, arrived):
    half = table.shape[1]
    devices, own, rows = arrived.shape
    tile = min(1024, half)
    return pl.pallas_call(
        functools.partial(even_kernel, half=half),
        grid=(half // tile,),
        in_specs=[
            pl.BlockSpec((1, half, tile), lambda t: (0, 0, t)),
            pl.BlockSpec((devices, own, rows), lambda t: (0, 0, 0)),
        ],
        out_specs=pl.BlockSpec((rows, tile), lambda t: (0, t)),
        out_shape=jax.ShapeDtypeStruct((rows, half), jnp.float32),
        scratch_shapes=[pltpu.VMEM((rows, half), jnp.bfloat16)],
        compiler_params=pltpu.CompilerParams(vmem_limit_bytes=60 << 20),
        name="restore_even",
    )(table, arrived)


def odd_kernel(table, arrived, even, mirror, out, turned, *, half, tile):
    step = pl.program_id(0)

    @pl.when(step == 0)
    def _():
        rows = arrived.shape[2]
        turned[...] = turn(arrived[...].reshape(half, rows))

    odd = dot(turned[...], table[0])
    out[:, pl.ds(pl.multiple_of(step * tile, tile), tile)] = even[...] + odd
    left = even[...] - odd
    base = pl.multiple_of(2 * half - tile - step * tile, tile)
    for at in range(0, tile, lane_block):
        rest = left[:, at : at + lane_block]
        back = jnp.zeros_like(rest)
        for _ in range(3):
            piece = rest.astype(jnp.bfloat16)
            back += dot(piece, mirror[...])
            rest = rest - piece.astype(jnp.float32)
        out[:, pl.ds(base + tile - lane_block - at, lane_block)] = back


def restore(table, arrived, even, mirror):
    half = table.shape[1]
    devices, own, rows = arrived.shape
    tile = min(1024, half)
    return pl.pallas_call(
        functools.partial(odd_kernel, half=half, tile=tile),
        grid=(half // tile,),
        in_specs=[
            pl.BlockSpec((1, half, tile), lambda t: (1, 0, t)),
            pl.BlockSpec((devices, own, rows), lambda t: (0, 0, 0)),
            pl.BlockSpec((rows, tile), lambda t: (0, t)),
            pl.BlockSpec((lane_block, lane_block), lambda t: (0, 0)),
        ],
        out_specs=pl.BlockSpec((rows, 2 * half), lambda t: (0, 0)),
        out_shape=jax.ShapeDtypeStruct((rows, 2 * half), jnp.float32),
        scratch_shapes=[pltpu.VMEM((rows, half), jnp.bfloat16)],
        compiler_params=pltpu.CompilerParams(vmem_limit_bytes=60 << 20),
        name="restore",
    )(table, arrived, even, mirror)


def program(slices, otf_rows, otf_cols):
    axes = ("focus", "strip")
    focus_count = lax.axis_size("focus")
    devices = focus_count * lax.axis_size("strip")
    _, length = slices.shape[1:]
    half = length // 2
    piece = length // devices
    blocks = length // lane_block
    per = lane_block // piece
    above, below = edge_rows(slices, 4)
    table = cosine_halves(length)
    weights = band()
    mirror = exchange_matrix()
    focus = lax.axis_index("focus")
    owner = focus * lax.axis_size("strip") + lax.axis_index("strip")
    own = half // devices
    rows_response = otf_rows.reshape(half, 2).T.reshape(2, 1, half)
    local_cols = lax.dynamic_slice_in_dim(otf_cols, owner * 2 * own, 2 * own, 0).reshape(own, 2).T.reshape(2, own, 1)
    above, below, table, rows_response, local_cols, mirror, weights = lax.optimization_barrier(
        (above, below, table, rows_response, local_cols, mirror, weights)
    )
    ends = jnp.pad(above, ((0, 0), (12, 0), (0, 0))) + jnp.pad(below, ((0, 0), (0, 12), (0, 0)))
    chunks = row_chunks if per == 1 and piece % (16 * row_chunks) == 0 else 1
    chunk_rows = piece // chunks
    swap = [(i, focus_count - 1 - i) for i in range(focus_count)]

    def sums(ends, half_index, chunk, rows):
        place = (half_index * piece + chunk * chunk_rows) // math.gcd(128, rows)
        return stencil(place.astype(jnp.int32).reshape(1), slices, ends, weights, rows)

    last = []

    def exchange(values):
        if last:
            values, _ = lax.optimization_barrier((values, last[-1]))
        last.append(lax.all_to_all(values, axes, split_axis=0, concat_axis=0, tiled=True))
        return last[-1]

    received = lax.ppermute(sums(ends, focus_count - 1 - focus, 0, piece), "focus", swap)
    arrived = ([], [])
    for chunk in range(chunks):
        own_sums = sums(ends, focus, chunk, chunk_rows)
        folded = merge(own_sums, received, mirror, chunk * chunk_rows)
        for parities in ((0,), (1,)) if chunk == chunks - 1 else ((0, 1),):
            along = transform_rows(table, folded, parities, devices)
            if chunk < chunks - 1:
                ends, along = lax.optimization_barrier((ends, along))
            moved = exchange(along)
            for at, parity in enumerate(parities):
                arrived[parity].append((moved, at))
    strips = devices // focus_count
    order = [b % focus_count * strips + b // focus_count if per == 1 else b for b in range(blocks)]
    restored = []
    for parity in range(2):
        parts = arrived[parity]
        if per > 1:
            parts = [
                (
                    part.reshape(focus_count, devices // focus_count, own, piece)
                    .transpose(1, 0, 2, 3)
                    .reshape(blocks, per, own, piece)
                    .transpose(0, 2, 1, 3)
                    .reshape(blocks, 1, own, lane_block),
                    0,
                )
                for part, _ in parts
            ]
        back = filter_columns(table, rows_response, local_cols[parity], mirror, parts, order)
        if per > 1:
            back = back.reshape(blocks, own, per, piece).transpose(0, 2, 1, 3).reshape(devices, own, piece)
        restored.append(exchange(back))
    even = restore_even(table, restored[0])
    return restore(table, restored[1], even, mirror)


def solution(mesh):
    in_specs = (P(("field", "focus"), "strip", None), P(), P())
    out_specs = P(("field", "focus", "strip"), None)
    return jax.shard_map(program, mesh=mesh, in_specs=in_specs, out_specs=out_specs, check_vma=False)
```

```python
import functools
import math

import jax
import jax.numpy as jnp
from jax import lax
from jax.experimental import pallas as pl
from jax.experimental.pallas import tpu as pltpu
from jax.sharding import PartitionSpec as P


floor_weight = 0.01
noise_ratio = 0.01
lane_block = 256
row_chunks = 2


def dot(left, right):
    return jnp.dot(left, right, preferred_element_type=jnp.float32)


def dot_last(left, right):
    return lax.dot_general(left, right, (((1,), (1,)), ((), ())), preferred_element_type=jnp.float32)


def edge_rows(slices, width):
    count = lax.axis_size("strip")
    ends = count - 1
    head = slices[:, :width, :]
    tail = slices[:, slices.shape[1] - width :, :]
    above = lax.ppermute(tail, "strip", [(i, i + 1) for i in range(ends)])
    below = lax.ppermute(head, "strip", [(i + 1, i) for i in range(ends)])
    return above, below


def band():
    source = lax.broadcasted_iota(jnp.int32, (256, 512), 0)
    column = lax.broadcasted_iota(jnp.int32, (256, 512), 1)
    which = column // 128
    offset = source - column % 128 - 64
    spacing = jnp.where(which == 0, 1, jnp.where(which == 1, 2, 4))
    lap = jnp.where(offset == 0, -4.0, jnp.where(jnp.abs(offset) == spacing, 1.0, 0.0))
    return jnp.where(which == 3, jnp.where(offset == 0, 1.0, 0.0), lap).astype(jnp.bfloat16)


def exchange_matrix():
    row = lax.broadcasted_iota(jnp.int32, (lane_block, lane_block), 0)
    column = lax.broadcasted_iota(jnp.int32, (lane_block, lane_block), 1)
    return (row + column == lane_block - 1).astype(jnp.bfloat16)


def stencil_kernel(
    place, main, above, below, ends, *rest, merging,
    tile_rows, count, cols, tiles, step, parts,
):
    if merging:
        received, folded, weights, edges, copies_a, copies_b, laps_a, laps_b, joined, out = rest
    else:
        out, weights, edges, copies_a, copies_b, laps_a, laps_b, joined = rest

    @pl.when(pl.program_id(0) == 0)
    def _():
        weights[...] = band()

    tile = place[0] + pl.program_id(0)
    first = tile == 0
    last = tile == tiles - 1
    edge_row = lax.broadcasted_iota(jnp.int32, (16, cols), 0)
    for s in range(count):
        upper = jnp.where(first, ends[s], above[s])
        lower = jnp.where(last, ends[s], below[s])
        edges[s] = jnp.where(edge_row < 8, lower, upper)
    frames = cols // 128 + 1
    copies = (copies_a, copies_b)
    laps = (laps_a, laps_b)

    def start_of(frame):
        return frame * 128 - 128 if isinstance(frame, int) else pl.multiple_of(frame * 128 - 128, 128)

    def window(source, frame, rows, low, high):
        size = (high - low) * rows
        if isinstance(frame, int) and frame == 0:
            piece = source[low:high, :, pl.ds(0, 128)].reshape(size, 128)
            return jnp.concatenate([jnp.zeros_like(piece), piece], axis=1)
        if isinstance(frame, int) and frame == frames - 1:
            piece = source[low:high, :, pl.ds(cols - 128, 128)].reshape(size, 128)
            return jnp.concatenate([piece, jnp.zeros_like(piece)], axis=1)
        return source[low:high, :, pl.ds(start_of(frame), 256)].reshape(size, 256)

    def spread_edges(slot, frame):
        rows = dot(window(edges, frame, 16, 0, count), weights[:, pl.ds(384, 128)])
        for s in range(count):
            copies[slot][s, pl.ds(0, 8), :] = rows[16 * s + 8 : 16 * s + 16]
            copies[slot][s, pl.ds(8 + tile_rows, 8), :] = rows[16 * s : 16 * s + 8]

    def spread(slot, frame, low, high):
        rows = dot(window(main, frame, tile_rows, low, high), weights[...])
        for s in range(low, high):
            at = (s - low) * tile_rows
            copies[slot][s, pl.ds(8, tile_rows), :] = rows[at : at + tile_rows, 384:]
            for k in range(3):
                laps[slot][s, k] = rows[at : at + tile_rows, 128 * k : 128 * k + 128]

    def gather(slot, frame, low, high):
        for r in range(low, high, step):
            numerator = denominator = None
            for s in range(count):
                centers = copies[slot]

                def lap(k, d):
                    pair = centers[s, pl.ds(8 + r + d, step), :] + centers[s, pl.ds(8 + r - d, step), :]
                    return laps[slot][s, k, pl.ds(r, step), :] + pair

                fine, middle, coarse = lap(0, 1), lap(1, 2), lap(2, 4)
                weight = floor_weight + (
                    fine * fine + 0.5 * (middle * middle + 0.5 * (coarse * coarse))
                )
                weighted = weight * centers[s, pl.ds(8 + r, step), :]
                numerator = weighted if s == 0 else numerator + weighted
                denominator = weight if s == 0 else denominator + weight
            joined[0, frame, pl.ds(r, step), :] = numerator
            joined[1, frame, pl.ds(r, step), :] = denominator

    def both(slot, frame):
        spread_edges(slot, frame)
        for q in range(parts):
            spread(slot, frame, q * count // parts, (q + 1) * count // parts)
            gather(1 - slot, frame - 1, q * tile_rows // parts, (q + 1) * tile_rows // parts)

    spread_edges(0, 0)
    spread(0, 0, 0, count)
    both(1, 1)
    both(0, 2)

    def two(i, carry):
        both(1, 2 * i + 1)
        both(0, 2 * i + 2)
        return carry

    lax.fori_loop(1, frames // 2 - 1, two, 0)
    both(1, frames - 2)
    both(0, frames - 1)
    gather(0, frames - 1, 0, tile_rows)
    lane = lax.broadcasted_iota(jnp.int32, (tile_rows, 128), 1)

    def shift_back(j, carry):
        at = pl.ds(pl.multiple_of(j * 128, 128), 128)
        for k in range(2):
            out[k, :, at] = pltpu.roll(jnp.where(lane >= 64, joined[k, j], joined[k, j + 1]), 64, 1)
        return carry

    lax.fori_loop(0, frames - 1, shift_back, 0)
    if merging:
        fold(out, received, folded)


def stencil(place, slices, ends, out_rows, received=None, at=0):
    count, rows, cols = slices.shape
    tile_rows = math.gcd(128, out_rows)
    per = tile_rows // 16
    blocks = rows // 16
    step = min(16, tile_rows)
    parts = 1
    merging = received is not None
    kernel = functools.partial(
        stencil_kernel, merging=merging, tile_rows=tile_rows, count=count, cols=cols, tiles=rows // tile_rows, step=step, parts=parts
    )
    edge = (count, 16, cols)
    width, kind = (cols // 2, jnp.bfloat16) if merging else (cols, jnp.float32)
    grid_spec = pltpu.PrefetchScalarGridSpec(
        num_scalar_prefetch=1,
        grid=(out_rows // tile_rows,),
        in_specs=[
            pl.BlockSpec((count, tile_rows, cols), lambda t, at: (0, at[0] + t, 0)),
            pl.BlockSpec(edge, lambda t, at: (0, jnp.maximum((at[0] + t) * per - 1, 0), 0)),
            pl.BlockSpec(edge, lambda t, at: (0, jnp.minimum((at[0] + t) * per + per, blocks - 1), 0)),
            pl.BlockSpec(edge, lambda t, at: (0, 0, 0)),
        ]
        + [pl.BlockSpec((2, tile_rows, cols), lambda t, place: (0, at // tile_rows + t, 0))] * merging,
        out_specs=pl.BlockSpec((2, tile_rows, width), lambda t, at: (0, t, 0)),
        scratch_shapes=[
            pltpu.VMEM((256, 512), jnp.bfloat16),
            pltpu.VMEM(edge, jnp.bfloat16),
            pltpu.VMEM((count, tile_rows + 16, 128), jnp.float32),
            pltpu.VMEM((count, tile_rows + 16, 128), jnp.float32),
            pltpu.VMEM((count, 3, tile_rows, 128), jnp.float32),
            pltpu.VMEM((count, 3, tile_rows, 128), jnp.float32),
            pltpu.VMEM((2, cols // 128 + 1, tile_rows, 128), jnp.float32),
        ]
        + [pltpu.VMEM((2, tile_rows, cols), jnp.float32)] * merging,
    )
    pixels = count * out_rows * cols
    return pl.pallas_call(
        kernel,
        grid_spec=grid_spec,
        out_shape=jax.ShapeDtypeStruct((2, out_rows, width), kind),
        cost_estimate=pl.CostEstimate(flops=pixels * 2048, bytes_accessed=pixels * 3, transcendentals=0),
        compiler_params=pltpu.CompilerParams(vmem_limit_bytes=60 << 20),
        name="stencil",
    )(place, slices, slices, slices, ends, *((received,) * merging))


def table_kernel(near_cos, near_sin, step_cos, step_sin, turn_cos, turn_sin, out, *, half):
    parity, block = pl.program_id(0), pl.program_id(1)
    period = near_cos.shape[1]
    group = min(64, period)
    norm = math.sqrt(1.0 / half)

    def fill(b, carry):
        for at in range(0, period, group):
            near = near_cos[0, pl.ds(at, group), :], near_sin[0, pl.ds(at, group), :]
            step = step_cos[0, pl.ds(at, group), :], step_sin[0, pl.ds(at, group), :]
            low_cos = near[0] * turn_cos[b] - near[1] * turn_sin[b]
            low_sin = near[1] * turn_cos[b] + near[0] * turn_sin[b]
            row = at + lax.broadcasted_iota(jnp.int32, low_cos.shape, 0)
            first = (row == 0) & (parity == 0) & (block == 0) & (b == 0)
            scale = jnp.where(first, norm * math.sqrt(0.5), norm)
            before = scale * low_cos
            here = scale * (step[0] * low_cos - step[1] * low_sin)
            twice = step[0] + step[0]
            rows = pl.ds(pl.multiple_of(b * period + at, group), group)
            out[0, rows, pl.ds(0, 128)] = before.astype(jnp.bfloat16)
            for j in range(1, half // 128):
                out[0, rows, pl.ds(j * 128, 128)] = here.astype(jnp.bfloat16)
                before, here = here, twice * here - before
        return carry

    lax.fori_loop(0, out.shape[1] // period, fill, 0)


def cosine_halves(length):
    half = length // 2
    rows = min(256, half)
    tall = min(1024, half)
    assert 512 * rows % (4 * length) == 0
    unit = jnp.float32(math.pi / (2 * length))

    def pair(phase):
        angle = (phase % (4 * length)).astype(jnp.float32) * unit
        return [jnp.cos(angle), jnp.sin(angle)]

    def iota(shape, dim):
        return lax.broadcasted_iota(jnp.int32, shape, dim)

    odd = (2, rows, 128)
    frequency = 2 * iota(odd, 1) + iota(odd, 0)
    near = pair((2 * iota(odd, 2) + 1) * frequency) + pair(256 * frequency)
    blocks = (half // rows, 1, 128)
    turn = pair((2 * iota(blocks, 2) + 1) * (2 * rows * iota(blocks, 0)))
    return pl.pallas_call(
        functools.partial(table_kernel, half=half),
        grid=(2, half // tall),
        in_specs=[
            pl.BlockSpec((1, rows, 128), lambda p, b: (p, 0, 0)),
        ]
        * 4
        + [pl.BlockSpec((tall // rows, 1, 128), lambda p, b: (b, 0, 0))] * 2,
        out_specs=pl.BlockSpec((1, tall, half), lambda p, b: (p, b, 0)),
        out_shape=jax.ShapeDtypeStruct((2, half, half), jnp.bfloat16),
        name="cosines",
    )(*near, *turn)


def fold(own, other, out):
    cols = own.shape[2]
    mirror = exchange_matrix()

    def merged(at):
        numerator = own[0, :, pl.ds(at, lane_block)] + other[0, :, pl.ds(at, lane_block)]
        denominator = own[1, :, pl.ds(at, lane_block)] + other[1, :, pl.ds(at, lane_block)]
        return (numerator / denominator).astype(jnp.bfloat16)

    for at in range(0, cols // 2, lane_block):
        near = merged(at).astype(jnp.float32)
        far = dot(merged(cols - lane_block - at), mirror)
        out[0, :, pl.ds(at, lane_block)] = (near + far).astype(jnp.bfloat16)
        out[1, :, pl.ds(at, lane_block)] = (near - far).astype(jnp.bfloat16)


def merge(own, other, at):
    _, rows, cols = own.shape
    tile = min(64, rows)
    first = at // tile
    return pl.pallas_call(
        fold,
        grid=(rows // tile,),
        in_specs=[
            pl.BlockSpec((2, tile, cols), lambda t: (0, t, 0)),
            pl.BlockSpec((2, tile, cols), lambda t: (0, first + t, 0)),
        ],
        out_specs=pl.BlockSpec((2, tile, cols // 2), lambda t: (0, t, 0)),
        out_shape=jax.ShapeDtypeStruct((2, rows, cols // 2), jnp.bfloat16),
        name="merge",
    )(own, other)


def rows_kernel(table, folded, out):
    values = dot_last(table[0], folded[0]).astype(jnp.bfloat16)
    out[...] = values.reshape(out.shape)


def transform_rows(table, folded, parities, devices):
    _, rows, half = folded.shape
    own = half // devices
    tile = max(1024, own)
    first = parities[0]
    return pl.pallas_call(
        rows_kernel,
        grid=(len(parities), half // tile),
        in_specs=[
            pl.BlockSpec((1, tile, half), lambda p, t: (first + p, t, 0)),
            pl.BlockSpec((1, rows, half), lambda p, t: (first + p, 0, 0)),
        ],
        out_specs=pl.BlockSpec((tile // own, 1, own, rows), lambda p, t: (t, p, 0, 0)),
        out_shape=jax.ShapeDtypeStruct((devices, len(parities), own, rows), jnp.bfloat16),
        name="transform_rows",
    )(table, folded)


def columns_kernel(*refs, chunks, half, order):
    table, rows_response, cols_response = refs[:3]
    arrived = refs[3 : 3 + chunks]
    out, folded, total = refs[3 + chunks :]
    parity = pl.program_id(0)
    step = pl.program_id(1)
    blocks = half // lane_block

    @pl.when((parity == 0) & (step == 0))
    def _():
        mirror = exchange_matrix()
        for j in range(blocks):
            near = jnp.concatenate([part[order[j], 0] for part in arrived], axis=1).astype(jnp.float32)
            far = dot(
                jnp.concatenate([part[order[2 * blocks - 1 - j], 0] for part in arrived], axis=1), mirror
            )
            folded[0, :, pl.ds(j * lane_block, lane_block)] = (near + far).astype(jnp.bfloat16)
            folded[1, :, pl.ds(j * lane_block, lane_block)] = (near - far).astype(jnp.bfloat16)

    spectrum = dot_last(folded[parity], table[0])
    response = cols_response[...] * rows_response[0]
    filtered = (spectrum * (response / (response * response + noise_ratio))).astype(jnp.bfloat16)
    part = dot(filtered, table[0])

    @pl.when(step == 0)
    def _():
        total[parity] = part

    @pl.when(step > 0)
    def _():
        total[parity] += part

    @pl.when((parity == 1) & (step == pl.num_programs(1) - 1))
    def _():
        mirror = exchange_matrix()
        for j in range(blocks):
            even = total[0, :, pl.ds(j * lane_block, lane_block)]
            odd = total[1, :, pl.ds(j * lane_block, lane_block)]
            out[j] = (even + odd).astype(jnp.bfloat16)
            out[2 * blocks - 1 - j] = dot((even - odd).astype(jnp.bfloat16), mirror).astype(jnp.bfloat16)


def filter_columns(table, rows_response, cols_response, arrived, order):
    half = table.shape[1]
    blocks, _, own, _ = arrived[0][0].shape
    tile = min(1024, half)
    chunks = len(arrived)

    def whole(part, parity):
        return pl.BlockSpec((blocks, 1, own, part.shape[3]), lambda p, t: (0, parity, 0, 0))

    return pl.pallas_call(
        functools.partial(columns_kernel, chunks=chunks, half=half, order=order),
        grid=(2, half // tile),
        in_specs=[
            pl.BlockSpec((1, tile, half), lambda p, t: (p, t, 0)),
            pl.BlockSpec((1, 1, tile), lambda p, t: (p, 0, t)),
            pl.BlockSpec((own, 1), lambda p, t: (0, 0)),
        ]
        + [whole(*pair) for pair in arrived],
        out_specs=pl.BlockSpec((blocks, own, lane_block), lambda p, t: (0, 0, 0)),
        out_shape=jax.ShapeDtypeStruct((blocks, own, lane_block), jnp.bfloat16),
        scratch_shapes=[
            pltpu.VMEM((2, own, half), jnp.bfloat16),
            pltpu.VMEM((2, own, half), jnp.float32),
        ],
        compiler_params=pltpu.CompilerParams(vmem_limit_bytes=60 << 20),
        name="filter_columns",
    )(table, rows_response, cols_response, *(part for part, _ in arrived))


def turn(values):
    return jnp.transpose(values.astype(jnp.float32)).astype(jnp.bfloat16)


def even_kernel(table, arrived, out, turned, *, half):
    @pl.when(pl.program_id(0) == 0)
    def _():
        rows = arrived.shape[2]
        turned[...] = turn(arrived[...].reshape(half, rows))

    out[...] = dot(turned[...], table[0])


def restore_even(table, arrived):
    half = table.shape[1]
    devices, own, rows = arrived.shape
    tile = min(1024, half)
    return pl.pallas_call(
        functools.partial(even_kernel, half=half),
        grid=(half // tile,),
        in_specs=[
            pl.BlockSpec((1, half, tile), lambda t: (0, 0, t)),
            pl.BlockSpec((devices, own, rows), lambda t: (0, 0, 0)),
        ],
        out_specs=pl.BlockSpec((rows, tile), lambda t: (0, t)),
        out_shape=jax.ShapeDtypeStruct((rows, half), jnp.float32),
        scratch_shapes=[pltpu.VMEM((rows, half), jnp.bfloat16)],
        compiler_params=pltpu.CompilerParams(vmem_limit_bytes=60 << 20),
        name="restore_even",
    )(table, arrived)


def odd_kernel(table, arrived, even, out, turned, *, half, tile):
    step = pl.program_id(0)

    @pl.when(step == 0)
    def _():
        rows = arrived.shape[2]
        turned[...] = turn(arrived[...].reshape(half, rows))

    odd = dot(turned[...], table[0])
    out[:, pl.ds(pl.multiple_of(step * tile, tile), tile)] = even[...] + odd
    left = even[...] - odd
    mirror = exchange_matrix()
    base = pl.multiple_of(2 * half - tile - step * tile, tile)
    for at in range(0, tile, lane_block):
        rest = left[:, at : at + lane_block]
        back = jnp.zeros_like(rest)
        for _ in range(3):
            piece = rest.astype(jnp.bfloat16)
            back += dot(piece, mirror)
            rest = rest - piece.astype(jnp.float32)
        out[:, pl.ds(base + tile - lane_block - at, lane_block)] = back


def restore(table, arrived, even):
    half = table.shape[1]
    devices, own, rows = arrived.shape
    tile = min(1024, half)
    return pl.pallas_call(
        functools.partial(odd_kernel, half=half, tile=tile),
        grid=(half // tile,),
        in_specs=[
            pl.BlockSpec((1, half, tile), lambda t: (1, 0, t)),
            pl.BlockSpec((devices, own, rows), lambda t: (0, 0, 0)),
            pl.BlockSpec((rows, tile), lambda t: (0, t)),
        ],
        out_specs=pl.BlockSpec((rows, 2 * half), lambda t: (0, 0)),
        out_shape=jax.ShapeDtypeStruct((rows, 2 * half), jnp.float32),
        scratch_shapes=[pltpu.VMEM((rows, half), jnp.bfloat16)],
        compiler_params=pltpu.CompilerParams(vmem_limit_bytes=60 << 20),
        name="restore",
    )(table, arrived, even)


def program(slices, otf_rows, otf_cols):
    axes = ("focus", "strip")
    focus_count = lax.axis_size("focus")
    devices = focus_count * lax.axis_size("strip")
    _, length = slices.shape[1:]
    half = length // 2
    piece = length // devices
    blocks = length // lane_block
    per = lane_block // piece
    above, below = edge_rows(slices, 4)
    table = cosine_halves(length)
    focus = lax.axis_index("focus")
    owner = focus * lax.axis_size("strip") + lax.axis_index("strip")
    own = half // devices
    above, below, table = lax.optimization_barrier((above, below, table))
    ends = jnp.pad(above, ((0, 0), (12, 0), (0, 0))) + jnp.pad(below, ((0, 0), (0, 12), (0, 0)))
    chunks = row_chunks if per == 1 and piece % (16 * row_chunks) == 0 else 1
    chunk_rows = piece // chunks
    swap = [(i, focus_count - 1 - i) for i in range(focus_count)]

    def sums(ends, half_index, chunk, rows, *merging):
        place = (half_index * piece + chunk * chunk_rows) // math.gcd(128, rows)
        return stencil(place.astype(jnp.int32).reshape(1), slices, ends, rows, *merging)

    last = []

    def exchange(values):
        if last:
            values, _ = lax.optimization_barrier((values, last[-1]))
        last.append(lax.all_to_all(values, axes, split_axis=0, concat_axis=0, tiled=True))
        return last[-1]

    def responses():
        local = lax.dynamic_slice_in_dim(otf_cols, owner * 2 * own, 2 * own, 0)
        return otf_rows.reshape(half, 2).T.reshape(2, 1, half), local.reshape(own, 2).T.reshape(2, own, 1)

    received = lax.ppermute(sums(ends, focus_count - 1 - focus, 0, piece), "focus", swap)
    arrived = ([], [])
    for chunk in range(chunks):
        if chunk == 0:
            folded = merge(sums(ends, focus, 0, chunk_rows), received, 0)
        else:
            folded = sums(ends, focus, chunk, chunk_rows, received, chunk * chunk_rows)
        for parities in ((0,), (1,)) if chunk == chunks - 1 else ((0, 1),):
            along = transform_rows(table, folded, parities, devices)
            if chunk < chunks - 1:
                ends, along = lax.optimization_barrier((ends, along))
            elif parities == (0,):
                otf_rows, otf_cols, along = lax.optimization_barrier((otf_rows, otf_cols, along))
                rows_response, local_cols = responses()
            else:
                along, rows_response, local_cols = lax.optimization_barrier((along, rows_response, local_cols))
            moved = exchange(along)
            for at, parity in enumerate(parities):
                arrived[parity].append((moved, at))
    strips = devices // focus_count
    order = [b % focus_count * strips + b // focus_count if per == 1 else b for b in range(blocks)]
    restored = []
    for parity in range(2):
        parts = arrived[parity]
        if per > 1:
            parts = [
                (
                    part.reshape(focus_count, devices // focus_count, own, piece)
                    .transpose(1, 0, 2, 3)
                    .reshape(blocks, per, own, piece)
                    .transpose(0, 2, 1, 3)
                    .reshape(blocks, 1, own, lane_block),
                    0,
                )
                for part, _ in parts
            ]
        back = filter_columns(table, rows_response, local_cols[parity], parts, order)
        if per > 1:
            back = back.reshape(blocks, own, per, piece).transpose(0, 2, 1, 3).reshape(devices, own, piece)
        restored.append(exchange(back))
    even = restore_even(table, restored[0])
    return restore(table, restored[1], even)


def solution(mesh):
    in_specs = (P(("field", "focus"), "strip", None), P(), P())
    out_specs = P(("field", "focus", "strip"), None)
    return jax.shard_map(program, mesh=mesh, in_specs=in_specs, out_specs=out_specs, check_vma=False)
```

```python
import functools
import math

import jax
import jax.numpy as jnp
from jax import lax
from jax.experimental import pallas as pl
from jax.experimental.pallas import tpu as pltpu
from jax.sharding import PartitionSpec as P


floor_weight = 0.01
noise_ratio = 0.01
lane_block = 256
row_chunks = 2


def dot(left, right):
    return jnp.dot(left, right, preferred_element_type=jnp.float32)


def dot_last(left, right):
    return lax.dot_general(left, right, (((1,), (1,)), ((), ())), preferred_element_type=jnp.float32)


def edge_rows(slices, width):
    count = lax.axis_size("strip")
    ends = count - 1
    head = slices[:, :width, :]
    tail = slices[:, slices.shape[1] - width :, :]
    above = lax.ppermute(tail, "strip", [(i, i + 1) for i in range(ends)])
    below = lax.ppermute(head, "strip", [(i + 1, i) for i in range(ends)])
    return above, below


def band():
    source = lax.broadcasted_iota(jnp.int32, (256, 512), 0)
    column = lax.broadcasted_iota(jnp.int32, (256, 512), 1)
    which = column // 128
    offset = source - column % 128 - 64
    spacing = jnp.where(which == 0, 1, jnp.where(which == 1, 2, 4))
    lap = jnp.where(offset == 0, -4.0, jnp.where(jnp.abs(offset) == spacing, 1.0, 0.0))
    return jnp.where(which == 3, jnp.where(offset == 0, 1.0, 0.0), lap).astype(jnp.bfloat16)


def exchange_matrix():
    row = lax.broadcasted_iota(jnp.int32, (lane_block, lane_block), 0)
    column = lax.broadcasted_iota(jnp.int32, (lane_block, lane_block), 1)
    return (row + column == lane_block - 1).astype(jnp.bfloat16)


def stencil_kernel(
    place, main, above, below, ends, *rest, merging,
    tile_rows, count, cols, tiles, step, parts,
):
    if merging:
        received, folded, weights, edges, copies_a, copies_b, laps_a, laps_b, joined, out = rest
    else:
        out, weights, edges, copies_a, copies_b, laps_a, laps_b, joined = rest

    @pl.when(pl.program_id(0) == 0)
    def _():
        weights[...] = band()

    tile = place[0] + pl.program_id(0)
    first = tile == 0
    last = tile == tiles - 1
    edge_row = lax.broadcasted_iota(jnp.int32, (16, cols), 0)
    for s in range(count):
        upper = jnp.where(first, ends[s], above[s])
        lower = jnp.where(last, ends[s], below[s])
        edges[s] = jnp.where(edge_row < 8, lower, upper)
    frames = cols // 128 + 1
    copies = (copies_a, copies_b)
    laps = (laps_a, laps_b)

    def start_of(frame):
        return frame * 128 - 128 if isinstance(frame, int) else pl.multiple_of(frame * 128 - 128, 128)

    def window(source, frame, rows, low, high):
        size = (high - low) * rows
        if isinstance(frame, int) and frame == 0:
            piece = source[low:high, :, pl.ds(0, 128)].reshape(size, 128)
            return jnp.concatenate([jnp.zeros_like(piece), piece], axis=1)
        if isinstance(frame, int) and frame == frames - 1:
            piece = source[low:high, :, pl.ds(cols - 128, 128)].reshape(size, 128)
            return jnp.concatenate([piece, jnp.zeros_like(piece)], axis=1)
        return source[low:high, :, pl.ds(start_of(frame), 256)].reshape(size, 256)

    def spread_edges(slot, frame):
        rows = dot(window(edges, frame, 16, 0, count), weights[:, pl.ds(384, 128)])
        for s in range(count):
            copies[slot][s, pl.ds(0, 8), :] = rows[16 * s + 8 : 16 * s + 16]
            copies[slot][s, pl.ds(8 + tile_rows, 8), :] = rows[16 * s : 16 * s + 8]

    def spread(slot, frame, low, high):
        rows = dot(window(main, frame, tile_rows, low, high), weights[...])
        for s in range(low, high):
            at = (s - low) * tile_rows
            copies[slot][s, pl.ds(8, tile_rows), :] = rows[at : at + tile_rows, 384:]
            for k in range(3):
                laps[slot][s, k] = rows[at : at + tile_rows, 128 * k : 128 * k + 128]

    def gather(slot, frame, low, high):
        for r in range(low, high, step):
            numerator = denominator = None
            for s in range(count):
                centers = copies[slot]

                def lap(k, d):
                    pair = centers[s, pl.ds(8 + r + d, step), :] + centers[s, pl.ds(8 + r - d, step), :]
                    return laps[slot][s, k, pl.ds(r, step), :] + pair

                fine, middle, coarse = lap(0, 1), lap(1, 2), lap(2, 4)
                weight = floor_weight + (
                    fine * fine + 0.5 * (middle * middle + 0.5 * (coarse * coarse))
                )
                weighted = weight * centers[s, pl.ds(8 + r, step), :]
                numerator = weighted if s == 0 else numerator + weighted
                denominator = weight if s == 0 else denominator + weight
            joined[0, frame, pl.ds(r, step), :] = numerator
            joined[1, frame, pl.ds(r, step), :] = denominator

    def both(slot, frame):
        spread_edges(slot, frame)
        for q in range(parts):
            spread(slot, frame, q * count // parts, (q + 1) * count // parts)
            gather(1 - slot, frame - 1, q * tile_rows // parts, (q + 1) * tile_rows // parts)

    spread_edges(0, 0)
    spread(0, 0, 0, count)
    both(1, 1)
    both(0, 2)

    def two(i, carry):
        both(1, 2 * i + 1)
        both(0, 2 * i + 2)
        return carry

    lax.fori_loop(1, frames // 2 - 1, two, 0)
    both(1, frames - 2)
    both(0, frames - 1)
    gather(0, frames - 1, 0, tile_rows)
    lane = lax.broadcasted_iota(jnp.int32, (tile_rows, 128), 1)

    def shift_back(j, carry):
        at = pl.ds(pl.multiple_of(j * 128, 128), 128)
        for k in range(2):
            out[k, :, at] = pltpu.roll(jnp.where(lane >= 64, joined[k, j], joined[k, j + 1]), 64, 1)
        return carry

    lax.fori_loop(0, frames - 1, shift_back, 0)
    if merging:
        fold(out, received, folded)


def stencil(place, slices, ends, out_rows, received=None, at=0):
    count, rows, cols = slices.shape
    tile_rows = math.gcd(128, out_rows)
    per = tile_rows // 16
    blocks = rows // 16
    step = min(16, tile_rows)
    parts = 1
    merging = received is not None
    kernel = functools.partial(
        stencil_kernel, merging=merging, tile_rows=tile_rows, count=count, cols=cols, tiles=rows // tile_rows, step=step, parts=parts
    )
    edge = (count, 16, cols)
    width, kind = (cols // 2, jnp.bfloat16) if merging else (cols, jnp.float32)
    grid_spec = pltpu.PrefetchScalarGridSpec(
        num_scalar_prefetch=1,
        grid=(out_rows // tile_rows,),
        in_specs=[
            pl.BlockSpec((count, tile_rows, cols), lambda t, at: (0, at[0] + t, 0)),
            pl.BlockSpec(edge, lambda t, at: (0, jnp.maximum((at[0] + t) * per - 1, 0), 0)),
            pl.BlockSpec(edge, lambda t, at: (0, jnp.minimum((at[0] + t) * per + per, blocks - 1), 0)),
            pl.BlockSpec(edge, lambda t, at: (0, 0, 0)),
        ]
        + [pl.BlockSpec((2, tile_rows, cols), lambda t, place: (0, at // tile_rows + t, 0))] * merging,
        out_specs=pl.BlockSpec((2, tile_rows, width), lambda t, at: (0, t, 0)),
        scratch_shapes=[
            pltpu.VMEM((256, 512), jnp.bfloat16),
            pltpu.VMEM(edge, jnp.bfloat16),
            pltpu.VMEM((count, tile_rows + 16, 128), jnp.float32),
            pltpu.VMEM((count, tile_rows + 16, 128), jnp.float32),
            pltpu.VMEM((count, 3, tile_rows, 128), jnp.float32),
            pltpu.VMEM((count, 3, tile_rows, 128), jnp.float32),
            pltpu.VMEM((2, cols // 128 + 1, tile_rows, 128), jnp.float32),
        ]
        + [pltpu.VMEM((2, tile_rows, cols), jnp.float32)] * merging,
    )
    pixels = count * out_rows * cols
    return pl.pallas_call(
        kernel,
        grid_spec=grid_spec,
        out_shape=jax.ShapeDtypeStruct((2, out_rows, width), kind),
        cost_estimate=pl.CostEstimate(flops=pixels * 2048, bytes_accessed=pixels * 3, transcendentals=0),
        compiler_params=pltpu.CompilerParams(vmem_limit_bytes=60 << 20),
        name="stencil",
    )(place, slices, slices, slices, ends, *((received,) * merging))


def table_kernel(near_cos, near_sin, step_cos, step_sin, turn_cos, turn_sin, out, *, half):
    parity, block = pl.program_id(0), pl.program_id(1)
    period = near_cos.shape[1]
    group = min(64, period)
    norm = math.sqrt(1.0 / half)

    def fill(b, carry):
        for at in range(0, period, group):
            near = near_cos[0, pl.ds(at, group), :], near_sin[0, pl.ds(at, group), :]
            step = step_cos[0, pl.ds(at, group), :], step_sin[0, pl.ds(at, group), :]
            low_cos = near[0] * turn_cos[b] - near[1] * turn_sin[b]
            low_sin = near[1] * turn_cos[b] + near[0] * turn_sin[b]
            row = at + lax.broadcasted_iota(jnp.int32, low_cos.shape, 0)
            first = (row == 0) & (parity == 0) & (block == 0) & (b == 0)
            scale = jnp.where(first, norm * math.sqrt(0.5), norm)
            before = scale * low_cos
            here = scale * (step[0] * low_cos - step[1] * low_sin)
            twice = step[0] + step[0]
            rows = pl.ds(pl.multiple_of(b * period + at, group), group)
            out[0, rows, pl.ds(0, 128)] = before.astype(jnp.bfloat16)
            for j in range(1, half // 128):
                out[0, rows, pl.ds(j * 128, 128)] = here.astype(jnp.bfloat16)
                before, here = here, twice * here - before
        return carry

    lax.fori_loop(0, out.shape[1] // period, fill, 0)


def cosine_halves(length):
    half = length // 2
    rows = min(256, half)
    tall = min(1024, half)
    assert 512 * rows % (4 * length) == 0
    unit = jnp.float32(math.pi / (2 * length))

    def pair(phase):
        angle = (phase % (4 * length)).astype(jnp.float32) * unit
        return [jnp.cos(angle), jnp.sin(angle)]

    def iota(shape, dim):
        return lax.broadcasted_iota(jnp.int32, shape, dim)

    odd = (2, rows, 128)
    frequency = 2 * iota(odd, 1) + iota(odd, 0)
    near = pair((2 * iota(odd, 2) + 1) * frequency) + pair(256 * frequency)
    blocks = (half // rows, 1, 128)
    turn = pair((2 * iota(blocks, 2) + 1) * (2 * rows * iota(blocks, 0)))
    return pl.pallas_call(
        functools.partial(table_kernel, half=half),
        grid=(2, half // tall),
        in_specs=[
            pl.BlockSpec((1, rows, 128), lambda p, b: (p, 0, 0)),
        ]
        * 4
        + [pl.BlockSpec((tall // rows, 1, 128), lambda p, b: (b, 0, 0))] * 2,
        out_specs=pl.BlockSpec((1, tall, half), lambda p, b: (p, b, 0)),
        out_shape=jax.ShapeDtypeStruct((2, half, half), jnp.bfloat16),
        name="cosines",
    )(*near, *turn)


def fold(own, other, out):
    cols = own.shape[2]
    mirror = exchange_matrix()

    def merged(at):
        numerator = own[0, :, pl.ds(at, lane_block)] + other[0, :, pl.ds(at, lane_block)]
        denominator = own[1, :, pl.ds(at, lane_block)] + other[1, :, pl.ds(at, lane_block)]
        return (numerator / denominator).astype(jnp.bfloat16)

    for at in range(0, cols // 2, lane_block):
        near = merged(at).astype(jnp.float32)
        far = dot(merged(cols - lane_block - at), mirror)
        out[0, :, pl.ds(at, lane_block)] = (near + far).astype(jnp.bfloat16)
        out[1, :, pl.ds(at, lane_block)] = (near - far).astype(jnp.bfloat16)


def merge(own, other, at):
    _, rows, cols = own.shape
    tile = min(64, rows)
    first = at // tile
    return pl.pallas_call(
        fold,
        grid=(rows // tile,),
        in_specs=[
            pl.BlockSpec((2, tile, cols), lambda t: (0, t, 0)),
            pl.BlockSpec((2, tile, cols), lambda t: (0, first + t, 0)),
        ],
        out_specs=pl.BlockSpec((2, tile, cols // 2), lambda t: (0, t, 0)),
        out_shape=jax.ShapeDtypeStruct((2, rows, cols // 2), jnp.bfloat16),
        name="merge",
    )(own, other)


def rows_kernel(table, folded, out):
    values = dot_last(table[0], folded[0]).astype(jnp.bfloat16)
    out[...] = values.reshape(out.shape)


def transform_rows(table, folded, parities, devices):
    _, rows, half = folded.shape
    own = half // devices
    tile = max(1024, own)
    first = parities[0]
    return pl.pallas_call(
        rows_kernel,
        grid=(len(parities), half // tile),
        in_specs=[
            pl.BlockSpec((1, tile, half), lambda p, t: (first + p, t, 0)),
            pl.BlockSpec((1, rows, half), lambda p, t: (first + p, 0, 0)),
        ],
        out_specs=pl.BlockSpec((tile // own, 1, own, rows), lambda p, t: (t, p, 0, 0)),
        out_shape=jax.ShapeDtypeStruct((devices, len(parities), own, rows), jnp.bfloat16),
        name="transform_rows",
    )(table, folded)


def columns_kernel(*refs, chunks, half, order):
    table, rows_response, cols_response = refs[:3]
    arrived = refs[3 : 3 + chunks]
    out, folded, total = refs[3 + chunks :]
    parity = pl.program_id(0)
    step = pl.program_id(1)
    blocks = half // lane_block

    @pl.when((parity == 0) & (step == 0))
    def _():
        mirror = exchange_matrix()
        for j in range(blocks):
            near = jnp.concatenate([part[order[j], 0] for part in arrived], axis=1).astype(jnp.float32)
            far = dot(
                jnp.concatenate([part[order[2 * blocks - 1 - j], 0] for part in arrived], axis=1), mirror
            )
            folded[0, :, pl.ds(j * lane_block, lane_block)] = (near + far).astype(jnp.bfloat16)
            folded[1, :, pl.ds(j * lane_block, lane_block)] = (near - far).astype(jnp.bfloat16)

    spectrum = dot_last(folded[parity], table[0])
    response = cols_response[...] * rows_response[0]
    filtered = (spectrum * (response / (response * response + noise_ratio))).astype(jnp.bfloat16)
    part = dot(filtered, table[0])

    @pl.when(step == 0)
    def _():
        total[parity] = part

    @pl.when(step > 0)
    def _():
        total[parity] += part

    @pl.when((parity == 1) & (step == pl.num_programs(1) - 1))
    def _():
        mirror = exchange_matrix()
        for j in range(blocks):
            even = total[0, :, pl.ds(j * lane_block, lane_block)]
            odd = total[1, :, pl.ds(j * lane_block, lane_block)]
            out[j] = (even + odd).astype(jnp.bfloat16)
            out[2 * blocks - 1 - j] = dot((even - odd).astype(jnp.bfloat16), mirror).astype(jnp.bfloat16)


def filter_columns(table, rows_response, cols_response, arrived, order):
    half = table.shape[1]
    blocks, _, own, _ = arrived[0][0].shape
    tile = min(1024, half)
    chunks = len(arrived)

    def whole(part, parity):
        return pl.BlockSpec((blocks, 1, own, part.shape[3]), lambda p, t: (0, parity, 0, 0))

    return pl.pallas_call(
        functools.partial(columns_kernel, chunks=chunks, half=half, order=order),
        grid=(2, half // tile),
        in_specs=[
            pl.BlockSpec((1, tile, half), lambda p, t: (p, t, 0)),
            pl.BlockSpec((1, 1, tile), lambda p, t: (p, 0, t)),
            pl.BlockSpec((own, 1), lambda p, t: (0, 0)),
        ]
        + [whole(*pair) for pair in arrived],
        out_specs=pl.BlockSpec((blocks, own, lane_block), lambda p, t: (0, 0, 0)),
        out_shape=jax.ShapeDtypeStruct((blocks, own, lane_block), jnp.bfloat16),
        scratch_shapes=[
            pltpu.VMEM((2, own, half), jnp.bfloat16),
            pltpu.VMEM((2, own, half), jnp.float32),
        ],
        compiler_params=pltpu.CompilerParams(vmem_limit_bytes=40 << 20),
        name="filter_columns",
    )(table, rows_response, cols_response, *(part for part, _ in arrived))


def turn(values):
    return jnp.transpose(values.astype(jnp.float32)).astype(jnp.bfloat16)


def even_kernel(table, arrived, out, turned, *, half):
    @pl.when(pl.program_id(0) == 0)
    def _():
        rows = arrived.shape[2]
        turned[...] = turn(arrived[...].reshape(half, rows))

    out[...] = dot(turned[...], table[0])


def restore_even(table, arrived):
    half = table.shape[1]
    devices, own, rows = arrived.shape
    tile = min(1024, half)
    return pl.pallas_call(
        functools.partial(even_kernel, half=half),
        grid=(half // tile,),
        in_specs=[
            pl.BlockSpec((1, half, tile), lambda t: (0, 0, t)),
            pl.BlockSpec((devices, own, rows), lambda t: (0, 0, 0)),
        ],
        out_specs=pl.BlockSpec((rows, tile), lambda t: (0, t)),
        out_shape=jax.ShapeDtypeStruct((rows, half), jnp.float32),
        scratch_shapes=[pltpu.VMEM((rows, half), jnp.bfloat16)],
        compiler_params=pltpu.CompilerParams(vmem_limit_bytes=40 << 20),
        name="restore_even",
    )(table, arrived)


def odd_kernel(table, arrived, even, out, turned, *, half, tile):
    step = pl.program_id(0)

    @pl.when(step == 0)
    def _():
        rows = arrived.shape[2]
        turned[...] = turn(arrived[...].reshape(half, rows))

    odd = dot(turned[...], table[0])
    out[:, pl.ds(pl.multiple_of(step * tile, tile), tile)] = even[...] + odd
    left = even[...] - odd
    mirror = exchange_matrix()
    base = pl.multiple_of(2 * half - tile - step * tile, tile)
    for at in range(0, tile, lane_block):
        rest = left[:, at : at + lane_block]
        back = jnp.zeros_like(rest)
        for _ in range(3):
            piece = rest.astype(jnp.bfloat16)
            back += dot(piece, mirror)
            rest = rest - piece.astype(jnp.float32)
        out[:, pl.ds(base + tile - lane_block - at, lane_block)] = back


def restore(table, arrived, even):
    half = table.shape[1]
    devices, own, rows = arrived.shape
    tile = min(1024, half)
    return pl.pallas_call(
        functools.partial(odd_kernel, half=half, tile=tile),
        grid=(half // tile,),
        in_specs=[
            pl.BlockSpec((1, half, tile), lambda t: (1, 0, t)),
            pl.BlockSpec((devices, own, rows), lambda t: (0, 0, 0)),
            pl.BlockSpec((rows, tile), lambda t: (0, t)),
        ],
        out_specs=pl.BlockSpec((rows, 2 * half), lambda t: (0, 0)),
        out_shape=jax.ShapeDtypeStruct((rows, 2 * half), jnp.float32),
        scratch_shapes=[pltpu.VMEM((rows, half), jnp.bfloat16)],
        compiler_params=pltpu.CompilerParams(vmem_limit_bytes=40 << 20),
        name="restore",
    )(table, arrived, even)


def program(slices, otf_rows, otf_cols):
    axes = ("focus", "strip")
    focus_count = lax.axis_size("focus")
    devices = focus_count * lax.axis_size("strip")
    _, length = slices.shape[1:]
    half = length // 2
    piece = length // devices
    blocks = length // lane_block
    per = lane_block // piece
    above, below = edge_rows(slices, 4)
    table = cosine_halves(length)
    focus = lax.axis_index("focus")
    owner = focus * lax.axis_size("strip") + lax.axis_index("strip")
    own = half // devices
    above, below, table = lax.optimization_barrier((above, below, table))
    ends = jnp.pad(above, ((0, 0), (12, 0), (0, 0))) + jnp.pad(below, ((0, 0), (0, 12), (0, 0)))
    chunks = row_chunks if per == 1 and piece % (16 * row_chunks) == 0 else 1
    chunk_rows = piece // chunks
    swap = [(i, focus_count - 1 - i) for i in range(focus_count)]

    def sums(ends, half_index, chunk, rows, *merging):
        place = (half_index * piece + chunk * chunk_rows) // math.gcd(128, rows)
        return stencil(place.astype(jnp.int32).reshape(1), slices, ends, rows, *merging)

    last = []

    def exchange(values):
        if last:
            values, _ = lax.optimization_barrier((values, last[-1]))
        last.append(lax.all_to_all(values, axes, split_axis=0, concat_axis=0, tiled=True))
        return last[-1]

    def responses():
        local = lax.dynamic_slice_in_dim(otf_cols, owner * 2 * own, 2 * own, 0)
        return otf_rows.reshape(half, 2).T.reshape(2, 1, half), local.reshape(own, 2).T.reshape(2, own, 1)

    received = lax.ppermute(sums(ends, focus_count - 1 - focus, 0, piece), "focus", swap)
    arrived = ([], [])
    for chunk in range(chunks):
        if chunk == 0:
            folded = merge(sums(ends, focus, 0, chunk_rows), received, 0)
        else:
            folded = sums(ends, focus, chunk, chunk_rows, received, chunk * chunk_rows)
        for parities in ((0,), (1,)) if chunk == chunks - 1 else ((0, 1),):
            along = transform_rows(table, folded, parities, devices)
            if chunk < chunks - 1:
                ends, along = lax.optimization_barrier((ends, along))
            elif parities == (0,):
                otf_rows, otf_cols, along = lax.optimization_barrier((otf_rows, otf_cols, along))
                rows_response, local_cols = responses()
            else:
                along, rows_response, local_cols = lax.optimization_barrier((along, rows_response, local_cols))
            moved = exchange(along)
            for at, parity in enumerate(parities):
                arrived[parity].append((moved, at))
    strips = devices // focus_count
    order = [b % focus_count * strips + b // focus_count if per == 1 else b for b in range(blocks)]
    restored = []
    for parity in range(2):
        parts = arrived[parity]
        if per > 1:
            parts = [
                (
                    part.reshape(focus_count, devices // focus_count, own, piece)
                    .transpose(1, 0, 2, 3)
                    .reshape(blocks, per, own, piece)
                    .transpose(0, 2, 1, 3)
                    .reshape(blocks, 1, own, lane_block),
                    0,
                )
                for part, _ in parts
            ]
        back = filter_columns(table, rows_response, local_cols[parity], parts, order)
        if per > 1:
            back = back.reshape(blocks, own, per, piece).transpose(0, 2, 1, 3).reshape(devices, own, piece)
        restored.append(exchange(back))
    even = restore_even(table, restored[0])
    return restore(table, restored[1], even)


def solution(mesh):
    in_specs = (P(("field", "focus"), "strip", None), P(), P())
    out_specs = P(("field", "focus", "strip"), None)
    return jax.shard_map(program, mesh=mesh, in_specs=in_specs, out_specs=out_specs, check_vma=False)
```
